32 devices in a mesh: groups: 2 (over y), ctx: 4 (over z), head: 2 (over x), pair: 2 (over core).
Axes of the slice: x: 2, y: 2, z: 4, core: 2. Of those that a mesh axis runs over, the one named last changes fastest.
Arguments:
- query_suffix: bfloat16 [3072, 40, 128], P(('groups', 'ctx'), ('head', 'pair')), parts along dimension 0, may hold values from -9 to 9
- key_suffix: bfloat16 [3072, 8, 128], P(('groups', 'ctx'), ('head', 'pair')), parts along dimension 0, may hold values from -4 to 4
- value_suffix: bfloat16 [3072, 8, 128], P(('groups', 'ctx'), ('head', 'pair')), parts along dimension 0, may hold values from -6 to 6
- key_prefix: bfloat16 [1024, 8, 128], P(('groups', 'ctx', 'pair'), 'head'), parts along dimension 0, may hold values from -4 to 4
- value_prefix: bfloat16 [1024, 8, 128], P(('groups', 'ctx', 'pair'), 'head'), parts along dimension 0, may hold values from -6 to 6
- file_ids: int32 [3072], P(('groups', 'ctx')), parts along dimension 0, may hold values from 0 to 3, never falling along the last dimension, each value on 1 to 768 neighbouring positions
Outputs:
- attention: bfloat16 [3072, 40, 128], P(('groups', 'ctx'), ('head', 'pair')), parts along dimension 0
The draws below stay inside these ranges and needn't reach their ends.
There are 2 independent parts, one for each index of `groups`. The reference program is written for one: setup_inputs(seed, part) draws one part's arguments, and reference() takes and returns one part's arrays. A program takes and returns all parts, laid end to end along the dimension named above; each array names one. Nothing has to cross between parts.
Inputs may be any that keep to these rules, and one draw needn't show every extreme that they name: `file_ids`: file numbers never fall along the tokens; every file has 1 to 768 tokens, and one has exactly 768.
All inputs are finite; a program needn't handle non-finite values.
Results may differ from the reference program's by a relative error of at most 0.007.
Values may be sent and summed in bfloat16 or wider, within the bound.
No kernel may reach another device: no remote copies, remote signals or barrier semaphores. Data moves between devices by JAX's collectives and lax.ppermute only.
A program may use at most 64 MiB of HBM per device.

```python
import math
import jax
import jax.numpy as jnp
import numpy as np
from jax import lax

QH = 40
KVH = 8
HD = 128
S_DEV = 384
TOKENS = 1536
PREFIX = 512
FILES = 4
FILE_MOST = 768


def rough_field(key, shape):
    return jnp.clip(jax.random.normal(jax.random.fold_in(key, 5), shape, jnp.float32), -4.0, 4.0)


def draw_query_suffix(key, part):
    field = rough_field(jax.random.fold_in(key, 11), (TOKENS, QH, HD))
    return field.astype(jnp.bfloat16)


def draw_key_suffix(key, part):
    field = rough_field(jax.random.fold_in(key, 12), (TOKENS, KVH, HD))
    return field.astype(jnp.bfloat16)


def draw_key_prefix(key, part):
    field = rough_field(jax.random.fold_in(key, 13), (PREFIX, KVH, HD))
    return field.astype(jnp.bfloat16)


def steps_of(key, dims, pieces, low, high):
    gain = 1.0
    for dim, blocks in pieces:
        draws = jax.random.uniform(jax.random.fold_in(jax.random.fold_in(key, 6), dim), (blocks,), jnp.float32, low / len(pieces), high / len(pieces))
        gain = gain * jnp.repeat(jnp.exp(draws), dims[dim] // blocks).reshape((-1,) + (1,) * (len(dims) - 1 - dim))
    return gain


def profile(amount, total, reach, slope):
    portions = [(1 << 20) // math.isqrt(standing ** slope) + 1 for standing in range(2, amount + 1)]
    spare, counts = total - reach - (amount - 1), [1] * (amount - 1)
    while spare > 0:
        candidates = [i for i in range(amount - 1) if counts[i] < reach]
        whole, remaining = sum([portions[i] for i in candidates]), spare
        for i in candidates:
            addition = min(reach - counts[i], max(1, remaining * portions[i] // whole), spare)
            counts[i] = counts[i] + addition
            spare = spare - addition
    return np.array([reach] + counts)


def uneven(own_key, number_of, total, most, skew):
    if number_of == 2:
        one = jax.random.randint(own_key, (), max(1, total - most), min(most, total - 1) + 1)
        return jnp.stack([one, total - one])
    sizes = jnp.asarray(profile(number_of, total, most, skew), jnp.int32)
    couples = (number_of - 1) // 2
    donor, sink = sizes[1:1 + 2 * couples:2], sizes[2:2 + 2 * couples:2]
    room = jnp.minimum(donor - 1, most - sink)
    passed = jax.random.randint(jax.random.fold_in(own_key, 1), (couples,), 0, 1 << 20) % (room + 1)
    sizes = sizes.at[1:1 + 2 * couples:2].set(donor - passed).at[2:2 + 2 * couples:2].set(sink + passed)
    return sizes[jax.random.permutation(jax.random.fold_in(own_key, 2), number_of)]


def centred(rng, dims, width, reach, cuts=(), kind=jnp.bfloat16):
    factor_of = steps_of(rng, dims, cuts, -0.22, 0.18) if cuts else 1.0
    values = jax.random.normal(rng, dims, jnp.float32) * width * factor_of
    return jnp.minimum(jnp.maximum(values, -reach), reach).astype(kind)


def setup_inputs(seed: int = 0, part: int = 0) -> dict:
    key_list = jax.random.split(jax.random.key(seed), 7)
    part_keys = jax.random.split(jax.random.fold_in(key_list[6], part), 7)
    return {
        "query_suffix": draw_query_suffix(jax.random.fold_in(jax.random.fold_in(key_list[6], part), 71), part),
        "key_suffix": draw_key_suffix(jax.random.fold_in(jax.random.fold_in(key_list[6], part), 71), part),
        "value_suffix": centred(part_keys[2], (TOKENS, KVH, HD), 1.0, 6.0, ((0, 4), (1, 4))),
        "key_prefix": draw_key_prefix(jax.random.fold_in(jax.random.fold_in(key_list[6], part), 71), part),
        "value_prefix": centred(part_keys[4], (PREFIX, KVH, HD), 1.0, 6.0, ((0, 8), (1, 2))),
        "file_ids": jnp.searchsorted(jnp.cumsum(uneven(part_keys[5], FILES, TOKENS, FILE_MOST, 2)), jnp.arange(TOKENS), side="right").astype(jnp.int32),
    }


def reference(query_suffix, key_suffix, value_suffix, key_prefix, value_prefix, file_ids):
    group = QH // KVH
    scale = 1.0 / math.sqrt(HD)
    pad_keys = jnp.concatenate([jnp.zeros((FILE_MOST, KVH, HD), jnp.bfloat16), key_suffix], 0)
    pad_values = jnp.concatenate([jnp.zeros((FILE_MOST, KVH, HD), jnp.bfloat16), value_suffix], 0)
    pad_files = jnp.concatenate([jnp.full((FILE_MOST,), -1, jnp.int32), file_ids.astype(jnp.int32)], 0)
    pad_places = jnp.arange(-FILE_MOST, TOKENS, dtype=jnp.int32)
    window = FILE_MOST + S_DEV
    prefix_keys = key_prefix.astype(jnp.float32)
    prefix_values = value_prefix.astype(jnp.float32)

    def one_block(index):
        start = (index * S_DEV).astype(jnp.int32)
        queries = lax.dynamic_slice_in_dim(query_suffix, start, S_DEV, 0).reshape(S_DEV, KVH, group, HD).astype(jnp.float32)
        near_keys = lax.dynamic_slice_in_dim(pad_keys, start, window, 0).astype(jnp.float32)
        near_values = lax.dynamic_slice_in_dim(pad_values, start, window, 0).astype(jnp.float32)
        near_files = lax.dynamic_slice_in_dim(pad_files, start, window, 0)
        near_places = lax.dynamic_slice_in_dim(pad_places, start, window, 0)
        query_files = lax.dynamic_slice_in_dim(file_ids.astype(jnp.int32), start, S_DEV, 0)
        query_places = start + jnp.arange(S_DEV, dtype=jnp.int32)
        prefix_scores = jnp.einsum('sjgd,pjd->sjgp', queries, prefix_keys) * scale
        suffix_scores = jnp.einsum('sjgd,wjd->sjgw', queries, near_keys) * scale
        visible = (near_files[None, :] == query_files[:, None]) & (near_places[None, :] <= query_places[:, None]) & (near_places[None, :] >= 0)
        suffix_scores = jnp.where(visible[:, None, None, :], suffix_scores, jnp.float32(-1e+30))
        top = jnp.maximum(prefix_scores.max(-1), suffix_scores.max(-1))
        prefix_weights = jnp.exp(prefix_scores - top[..., None])
        suffix_weights = jnp.exp(suffix_scores - top[..., None])
        denominator = prefix_weights.sum(-1) + suffix_weights.sum(-1)
        numerator = jnp.einsum('sjgp,pjd->sjgd', prefix_weights.astype(jnp.bfloat16).astype(jnp.float32), prefix_values)
        numerator = numerator + jnp.einsum('sjgw,wjd->sjgd', suffix_weights.astype(jnp.bfloat16).astype(jnp.float32), near_values)
        return (numerator / denominator[..., None]).astype(jnp.bfloat16).reshape(S_DEV, QH, HD)
    blocks = lax.map(one_block, jnp.arange(TOKENS // S_DEV, dtype=jnp.int32))
    return blocks.reshape(TOKENS, QH, HD)
```

```python
import functools
import math

import jax
import jax.numpy as jnp
from jax import lax
from jax.experimental import pallas as pl
from jax.experimental.pallas import tpu as pltpu
from jax.sharding import PartitionSpec as P

HIDDEN = -1e30
TILE = 128
IDROWS = 16
F32 = jnp.float32
BF16 = jnp.bfloat16
NT = (((1,), (1,)), ((), ()))
VM = pl.BlockSpec(memory_space=pltpu.VMEM)


def passed_on(value):
    count = lax.axis_size("ctx")
    return lax.ppermute(value, "ctx", [(i, i + 1) for i in range(count - 1)])


def swapped(value, axis, bit):
    count = lax.axis_size(axis)
    return lax.ppermute(value, axis, [(i, i ^ bit) for i in range(count)])


def split_heads(src, first, rows, heads, wide, dst, at):
    wide[0 : rows * heads, :] = src[first : first + rows * heads, :].astype(F32)
    for head in range(heads):
        dst[head, at : at + rows, 0:TILE] = wide[pl.ds(head, rows, stride=heads), :].astype(BF16)


def id_column(ids, tile):
    return jnp.transpose(jnp.broadcast_to(ids[tile : tile + 1, :].astype(F32), (TILE, TILE)))


def id_row(ids, tile):
    return jnp.broadcast_to(ids[tile : tile + 1, :].astype(F32), (TILE, TILE))


def choose_kernel(kv_local, own_k, own_v, other_k, other_v, out, wide):
    positions = out.shape[0] // (4 * kv_local)
    heads = own_k.shape[0] // positions
    start = lax.axis_index("pair") * kv_local
    place = 0
    for mine, other in ((own_k, other_k), (own_v, other_v)):
        for slot, src in enumerate((mine, other)):
            wide[slot] = src[...].astype(F32)
        for head in range(kv_local):
            for slot in range(2):
                picked = wide[slot, pl.ds(start + head, positions, stride=heads), :]
                out[place : place + positions, :] = picked.astype(BF16)
                place += positions


def early_kernel(
    kv_local, rows, factor, q, k0, v0, k1, v1, ids, acc_out, stat_out, keys, vals, wide, bias
):
    tiles = rows // TILE
    group = q.shape[0] // kv_local
    split_heads(k1, 0, rows, kv_local, wide, keys, 0)
    split_heads(k0, 0, rows, kv_local, wide, keys, rows)
    split_heads(v1, 0, rows, kv_local, wide, vals, 0)
    split_heads(v0, 0, rows, kv_local, wide, vals, rows)
    vals[:, :, TILE:] = jnp.ones_like(vals[:, :, TILE:])
    back = v1[rows * kv_local : rows * kv_local + IDROWS, :]
    mine = ids[...]
    spot = lax.broadcasted_iota(jnp.int32, (TILE, TILE), 0)
    place = lax.broadcasted_iota(jnp.int32, (TILE, TILE), 1)
    for i in range(tiles):
        column = id_column(mine, i)
        for j in range(tiles):
            bias[i, :, j * TILE : (j + 1) * TILE] = jnp.where(
                column == id_row(back, j), 0.0, HIDDEN
            )
        for j in range(i + 1):
            seen = column == id_row(mine, j)
            if j == i:
                seen = seen & (place <= spot)
            at = rows + j * TILE
            bias[i, :, at : at + TILE] = jnp.where(seen, 0.0, HIDDEN)

    def one_head(head, _):
        kv = lax.div(head, group)
        for i in range(tiles):
            span = rows + (i + 1) * TILE
            queries = q[head, i * TILE : (i + 1) * TILE, :]
            scores = lax.dot_general(
                queries, keys[kv, 0:span, :], NT, preferred_element_type=F32
            )
            scores = scores + bias[i, :, 0:span]
            top = jnp.max(scores, axis=1, keepdims=True)
            weights = jnp.exp2((scores - top) * factor).astype(BF16)
            mixed = jnp.dot(weights, vals[kv, 0:span, :], preferred_element_type=F32)
            acc_out[head, i * TILE : (i + 1) * TILE, :] = mixed
            stat_out[head, i * TILE : (i + 1) * TILE, :] = jnp.broadcast_to(top, (TILE, TILE))
        return 0

    lax.fori_loop(0, q.shape[0], one_head, 0)


def late_kernel(kv_local, rows, factor, chunks, *refs):
    q, acc, stat, k2, v2, ids = refs[:6]
    prefix = refs[6 : 6 + chunks]
    out, keys, vals, wide, bias = refs[6 + chunks :]
    tiles = rows // TILE
    group = q.shape[0] // kv_local
    split_heads(k2, 0, rows, kv_local, wide, keys, 0)
    split_heads(v2, 0, rows, kv_local, wide, vals, 0)
    vals[:, :, TILE:] = jnp.ones_like(vals[:, :, TILE:])
    at = rows
    for chunk in prefix:
        size = 2 * kv_local * TILE
        for first in range(0, chunk.shape[0], size):
            for head in range(kv_local):
                low = first + head * TILE
                keys[head, at : at + TILE, :] = chunk[low : low + TILE, :]
                low = first + (kv_local + head) * TILE
                vals[head, at : at + TILE, 0:TILE] = chunk[low : low + TILE, :]
            at += TILE
    total = at
    back = v2[rows * kv_local : rows * kv_local + IDROWS, :]
    mine = ids[...]
    for i in range(tiles):
        column = id_column(mine, i)
        for j in range(i, tiles):
            bias[i, :, j * TILE : (j + 1) * TILE] = jnp.where(
                column == id_row(back, j), 0.0, HIDDEN
            )

    def one_head(head, _):
        kv = lax.div(head, group)
        for i in range(tiles):
            part = slice(i * TILE, (i + 1) * TILE)
            first = i * TILE
            queries = q[head, part, :]
            far = lax.dot_general(
                queries, keys[kv, first:rows, :], NT, preferred_element_type=F32
            )
            far = far + bias[i, :, first:rows]
            near = lax.dot_general(
                queries, keys[kv, rows:total, :], NT, preferred_element_type=F32
            )
            old = stat[head, part, 0:1]
            top = jnp.maximum(
                jnp.maximum(jnp.max(far, axis=1, keepdims=True), jnp.max(near, axis=1, keepdims=True)),
                old,
            )
            fade = jnp.exp2((old - top) * factor)
            far = jnp.exp2((far - top) * factor).astype(BF16)
            near = jnp.exp2((near - top) * factor).astype(BF16)
            mixed = (
                acc[head, part, :] * fade
                + jnp.dot(far, vals[kv, first:rows, :], preferred_element_type=F32)
                + jnp.dot(near, vals[kv, rows:total, :], preferred_element_type=F32)
            )
            out[head, part, :] = (mixed[:, 0:TILE] / mixed[:, TILE:]).astype(BF16)
        return 0

    lax.fori_loop(0, q.shape[0], one_head, 0)


def shards(query_suffix, key_suffix, value_suffix, key_prefix, value_prefix, file_ids):
    rows, qheads, width = query_suffix.shape
    kv_local = key_suffix.shape[1]
    factor = math.log2(math.e) / math.sqrt(width)
    count = lax.axis_size("ctx")
    queries = query_suffix.transpose(1, 0, 2)
    k0 = key_suffix.reshape(rows * kv_local, width)
    v0 = value_suffix.reshape(rows * kv_local, width)
    ids = jnp.pad((file_ids + 1).astype(BF16).reshape(rows // TILE, TILE), ((0, IDROWS - rows // TILE), (0, 0)))
    k1 = passed_on(k0)
    v1 = passed_on(jnp.concatenate([v0, ids]))
    kp = key_prefix.reshape(-1, width)
    vp = value_prefix.reshape(-1, width)
    kp_other = swapped(kp, "pair", 1)
    vp_other = swapped(vp, "pair", 1)
    positions = key_prefix.shape[0]
    mine = pl.pallas_call(
        functools.partial(choose_kernel, kv_local),
        out_shape=jax.ShapeDtypeStruct((4 * kv_local * positions, width), BF16),
        in_specs=[VM] * 4,
        out_specs=VM,
        scratch_shapes=[pltpu.VMEM((2,) + kp.shape, F32)],
        cost_estimate=pl.CostEstimate(flops=0, bytes_accessed=4 * kp.size * 2, transcendentals=0),
        name="choose",
    )(kp, vp, kp_other, vp_other)
    prefix = [mine]
    bit = 1
    while bit < count:
        prefix.append(swapped(jnp.concatenate(prefix) if len(prefix) > 1 else mine, "ctx", bit))
        bit *= 2
    k2 = passed_on(k1)
    v2 = passed_on(v1)
    wide_stats = 2 * TILE
    pairs = 2 * rows
    acc, stat = pl.pallas_call(
        functools.partial(early_kernel, kv_local, rows, factor),
        out_shape=(
            jax.ShapeDtypeStruct((qheads, rows, wide_stats), F32),
            jax.ShapeDtypeStruct((qheads, rows, TILE), F32),
        ),
        in_specs=[VM] * 6,
        out_specs=(VM, VM),
        scratch_shapes=[
            pltpu.VMEM((kv_local, pairs, width), BF16),
            pltpu.VMEM((kv_local, pairs, 2 * width), BF16),
            pltpu.VMEM((rows * kv_local, width), F32),
            pltpu.VMEM((rows // TILE, TILE, pairs), F32),
        ],
        cost_estimate=pl.CostEstimate(
            flops=4 * rows * qheads * pairs * width, bytes_accessed=4 * 2**20, transcendentals=rows * qheads * pairs
        ),
        name="early",
    )(queries, k0, v0, k1, v1, ids)
    spans = rows + 2 * positions * count
    out = pl.pallas_call(
        functools.partial(late_kernel, kv_local, rows, factor, len(prefix)),
        out_shape=jax.ShapeDtypeStruct((qheads, rows, width), BF16),
        in_specs=[VM] * (6 + len(prefix)),
        out_specs=VM,
        scratch_shapes=[
            pltpu.VMEM((kv_local, spans, width), BF16),
            pltpu.VMEM((kv_local, spans, 2 * width), BF16),
            pltpu.VMEM((rows * kv_local, width), F32),
            pltpu.VMEM((rows // TILE, TILE, rows), F32),
        ],
        cost_estimate=pl.CostEstimate(
            flops=4 * rows * qheads * spans * width, bytes_accessed=4 * 2**20, transcendentals=rows * qheads * spans
        ),
        name="late",
    )(queries, acc, stat, k2, v2, ids, *prefix)
    return out.transpose(1, 0, 2)


def solution(mesh):
    in_specs = (
        P(("groups", "ctx"), ("head", "pair"), None),
        P(("groups", "ctx"), ("head", "pair"), None),
        P(("groups", "ctx"), ("head", "pair"), None),
        P(("groups", "ctx", "pair"), "head", None),
        P(("groups", "ctx", "pair"), "head", None),
        P(("groups", "ctx")),
    )
    out_specs = P(("groups", "ctx"), ("head", "pair"), None)
    return jax.shard_map(shards, mesh=mesh, in_specs=in_specs, out_specs=out_specs, check_vma=False)
```

```python
import functools
import math

import jax
import jax.numpy as jnp
from jax import lax
from jax.experimental import pallas as pl
from jax.experimental.pallas import tpu as pltpu
from jax.sharding import PartitionSpec as P

HIDDEN = -1e30
TILE = 128
IDROWS = 16
CHUNK = 32
GRANT = 24 * 2**20
F32 = jnp.float32
BF16 = jnp.bfloat16
NT = (((1,), (1,)), ((), ()))
VM = pl.BlockSpec(memory_space=pltpu.VMEM)


def passed_on(value):
    count = lax.axis_size("ctx")
    return lax.ppermute(value, "ctx", [(i, i + 1) for i in range(count - 1)])


def swapped(value, axis, bit):
    count = lax.axis_size(axis)
    return lax.ppermute(value, axis, [(i, i ^ bit) for i in range(count)])


def one_head_rows(src, first, rows, heads, wide, head):
    if head == 0:
        wide[0 : rows * heads, :] = src[first : first + rows * heads, :].astype(F32)
    return wide[pl.ds(head, rows, stride=heads), :]


def place_keys(src, rows, heads, wide, keys, at):
    for head in range(heads):
        picked = one_head_rows(src, 0, rows, heads, wide, head)
        for j in range(0, rows, TILE):
            keys[head, :, at + j : at + j + TILE] = jnp.transpose(picked[j : j + TILE, :]).astype(BF16)


def place_values(src, rows, heads, wide, vals, at):
    for head in range(heads):
        vals[head, at : at + rows, 0:TILE] = one_head_rows(src, 0, rows, heads, wide, head).astype(BF16)


def id_column(ids, tile):
    return jnp.transpose(jnp.broadcast_to(ids[tile : tile + 1, :].astype(F32), (TILE, TILE)))


def id_row(ids, tile):
    return jnp.broadcast_to(ids[tile : tile + 1, :].astype(F32), (TILE, TILE))


def choose_kernel(kv_local, own_k, own_v, other_k, other_v, out, wide):
    positions = out.shape[0] // (4 * kv_local)
    heads = own_k.shape[0] // positions
    start = lax.axis_index("pair") * kv_local
    place = 0
    for mine, other in ((own_k, other_k), (own_v, other_v)):
        for slot, src in enumerate((mine, other)):
            wide[slot] = src[...].astype(F32)
        for head in range(kv_local):
            for slot in range(2):
                picked = wide[slot, pl.ds(start + head, positions, stride=heads), :]
                out[place : place + positions, :] = picked.astype(BF16)
                place += positions


def attend(q, keys, vals, masked, bias, factor, old, emit, scores, peaks, tops, weights):
    qheads, rows, width = q.shape
    total = keys.shape[2]
    group = qheads // keys.shape[0]

    def score(head, slot):
        found = jnp.dot(q[head], keys[head // group], preferred_element_type=F32)
        peak = None
        for j in range(0, total, TILE):
            piece = found[:, j : j + TILE]
            if j < masked:
                piece = piece + bias[:, j : j + TILE]
            scores[slot, :, j : j + TILE] = piece
            peak = piece if peak is None else jnp.maximum(peak, piece)
        peaks[slot] = peak

    def weigh(head, slot):
        for r in range(0, rows, CHUNK):
            part = slice(r, r + CHUNK)
            top = jnp.max(peaks[slot, part, :], axis=1, keepdims=True)
            top = jnp.broadcast_to(top, (CHUNK, TILE))
            if old is not None:
                top = jnp.maximum(top, old[head, part, :])
            tops[slot, part, :] = top
            for j in range(0, total, TILE):
                shifted = (scores[slot, part, j : j + TILE] - top) * factor
                weights[slot, part, j : j + TILE] = jnp.exp2(shifted).astype(BF16)

    def mix(head, slot):
        mixed = jnp.dot(weights[slot], vals[head // group], preferred_element_type=F32)
        emit(head, tops.at[slot], mixed)

    def step(head, slot):
        score(head + 1, 1 - slot)
        weigh(head, slot)
        mix(head - 1, 1 - slot)

    score(0, 0)
    score(1, 1)
    weigh(0, 0)
    trips = (qheads - 2) // 2

    def trip(index, _):
        head = 1 + 2 * index
        step(head, 1)
        step(head + 1, 0)
        return 0

    lax.fori_loop(0, trips, trip, 0)
    for head in range(1 + 2 * trips, qheads - 1):
        step(head, head % 2)
    last = qheads - 1
    weigh(last, last % 2)
    mix(last - 1, (last - 1) % 2)
    mix(last, last % 2)


def early_kernel(
    kv_local, rows, factor, q, k0, v0, k1, v1, ids, acc_out, stat_out, keys, vals, wide, bias, *room
):
    tiles = rows // TILE
    place_keys(k0, rows, kv_local, wide, keys, rows)
    place_keys(k1, rows, kv_local, wide, keys, 0)
    place_values(v0, rows, kv_local, wide, vals, rows)
    place_values(v1, rows, kv_local, wide, vals, 0)
    vals[:, :, TILE:] = jnp.ones_like(vals[:, :, TILE:])
    back = v1[rows * kv_local : rows * kv_local + IDROWS, :]
    mine = ids[...]
    spot = lax.broadcasted_iota(jnp.int32, (TILE, TILE), 0)
    place = lax.broadcasted_iota(jnp.int32, (TILE, TILE), 1)
    for i in range(tiles):
        column = id_column(mine, i)
        part = slice(i * TILE, (i + 1) * TILE)
        for j in range(tiles):
            bias[part, j * TILE : (j + 1) * TILE] = jnp.where(
                column == id_row(back, j), 0.0, HIDDEN
            )
            at = rows + j * TILE
            seen = column == id_row(mine, j)
            if j == i:
                seen = seen & (place <= spot)
            hidden = jnp.full((TILE, TILE), HIDDEN, F32)
            bias[part, at : at + TILE] = jnp.where(seen, 0.0, HIDDEN) if j <= i else hidden

    def emit(head, top, mixed):
        acc_out[head] = mixed
        stat_out[head] = top[...]

    attend(q, keys, vals, 2 * rows, bias, factor, None, emit, *room)


def late_kernel(kv_local, rows, factor, chunks, *refs):
    q, acc, stat, k2, v2, ids = refs[:6]
    prefix = refs[6 : 6 + chunks]
    out, keys, vals, wide, bias, *room = refs[6 + chunks :]
    tiles = rows // TILE
    place_keys(k2, rows, kv_local, wide, keys, 0)
    place_values(v2, rows, kv_local, wide, vals, 0)
    vals[:, :, TILE:] = jnp.ones_like(vals[:, :, TILE:])
    at = rows
    for chunk in prefix:
        size = 2 * kv_local * TILE
        for first in range(0, chunk.shape[0], size):
            for head in range(kv_local):
                low = first + head * TILE
                keys[head, :, at : at + TILE] = jnp.transpose(chunk[low : low + TILE, :])
                low = first + (kv_local + head) * TILE
                vals[head, at : at + TILE, 0:TILE] = chunk[low : low + TILE, :]
            at += TILE
    back = v2[rows * kv_local : rows * kv_local + IDROWS, :]
    mine = ids[...]
    for i in range(tiles):
        column = id_column(mine, i)
        for j in range(tiles):
            bias[i * TILE : (i + 1) * TILE, j * TILE : (j + 1) * TILE] = jnp.where(
                column == id_row(back, j), 0.0, HIDDEN
            )

    def emit(head, top, mixed):
        fade = jnp.exp2((stat[head] - top[...]) * factor)
        upper = acc[head, :, 0:TILE] * fade + mixed[:, 0:TILE]
        lower = acc[head, :, TILE:] * fade + mixed[:, TILE:]
        out[head] = (upper / lower).astype(BF16)

    attend(q, keys, vals, rows, bias, factor, stat, emit, *room)


def working_room(rows, total):
    return [
        pltpu.VMEM((2, rows, total), F32),
        pltpu.VMEM((2, rows, TILE), F32),
        pltpu.VMEM((2, rows, TILE), F32),
        pltpu.VMEM((2, rows, total), BF16),
    ]


def shards(query_suffix, key_suffix, value_suffix, key_prefix, value_prefix, file_ids):
    rows, qheads, width = query_suffix.shape
    kv_local = key_suffix.shape[1]
    factor = math.log2(math.e) / math.sqrt(width)
    count = lax.axis_size("ctx")
    queries = query_suffix.transpose(1, 0, 2)
    k0 = key_suffix.reshape(rows * kv_local, width)
    v0 = value_suffix.reshape(rows * kv_local, width)
    ids = jnp.pad((file_ids + 1).astype(BF16).reshape(rows // TILE, TILE), ((0, IDROWS - rows // TILE), (0, 0)))
    k1 = passed_on(k0)
    v1 = passed_on(jnp.concatenate([v0, ids]))
    kp = key_prefix.reshape(-1, width)
    vp = value_prefix.reshape(-1, width)
    kp_other = swapped(kp, "pair", 1)
    vp_other = swapped(vp, "pair", 1)
    positions = key_prefix.shape[0]
    mine = pl.pallas_call(
        functools.partial(choose_kernel, kv_local),
        out_shape=jax.ShapeDtypeStruct((4 * kv_local * positions, width), BF16),
        in_specs=[VM] * 4,
        out_specs=VM,
        scratch_shapes=[pltpu.VMEM((2,) + kp.shape, F32)],
        cost_estimate=pl.CostEstimate(flops=0, bytes_accessed=4 * kp.size * 2, transcendentals=0),
        compiler_params=pltpu.CompilerParams(vmem_limit_bytes=GRANT),
        name="choose",
    )(kp, vp, kp_other, vp_other)
    prefix = [mine]
    bit = 1
    while bit < count:
        prefix.append(swapped(jnp.concatenate(prefix) if len(prefix) > 1 else mine, "ctx", bit))
        bit *= 2
    k2 = passed_on(k1)
    v2 = passed_on(v1)
    wide_stats = 2 * TILE
    pairs = 2 * rows
    acc, stat = pl.pallas_call(
        functools.partial(early_kernel, kv_local, rows, factor),
        out_shape=(
            jax.ShapeDtypeStruct((qheads, rows, wide_stats), F32),
            jax.ShapeDtypeStruct((qheads, rows, TILE), F32),
        ),
        in_specs=[VM] * 6,
        out_specs=(VM, VM),
        scratch_shapes=[
            pltpu.VMEM((kv_local, width, pairs), BF16),
            pltpu.VMEM((kv_local, pairs, 2 * width), BF16),
            pltpu.VMEM((rows * kv_local, width), F32),
            pltpu.VMEM((rows, pairs), F32),
            *working_room(rows, pairs),
        ],
        cost_estimate=pl.CostEstimate(
            flops=4 * rows * qheads * pairs * width, bytes_accessed=4 * 2**20, transcendentals=rows * qheads * pairs
        ),
        compiler_params=pltpu.CompilerParams(vmem_limit_bytes=GRANT),
        name="early",
    )(queries, k0, v0, k1, v1, ids)
    spans = rows + 2 * positions * count
    out = pl.pallas_call(
        functools.partial(late_kernel, kv_local, rows, factor, len(prefix)),
        out_shape=jax.ShapeDtypeStruct((qheads, rows, width), BF16),
        in_specs=[VM] * (6 + len(prefix)),
        out_specs=VM,
        scratch_shapes=[
            pltpu.VMEM((kv_local, width, spans), BF16),
            pltpu.VMEM((kv_local, spans, 2 * width), BF16),
            pltpu.VMEM((rows * kv_local, width), F32),
            pltpu.VMEM((rows, rows), F32),
            *working_room(rows, spans),
        ],
        cost_estimate=pl.CostEstimate(
            flops=4 * rows * qheads * spans * width, bytes_accessed=4 * 2**20, transcendentals=rows * qheads * spans
        ),
        compiler_params=pltpu.CompilerParams(vmem_limit_bytes=GRANT),
        name="late",
    )(queries, acc, stat, k2, v2, ids, *prefix)
    return out.transpose(1, 0, 2)


def solution(mesh):
    in_specs = (
        P(("groups", "ctx"), ("head", "pair"), None),
        P(("groups", "ctx"), ("head", "pair"), None),
        P(("groups", "ctx"), ("head", "pair"), None),
        P(("groups", "ctx", "pair"), "head", None),
        P(("groups", "ctx", "pair"), "head", None),
        P(("groups", "ctx")),
    )
    out_specs = P(("groups", "ctx"), ("head", "pair"), None)
    return jax.shard_map(shards, mesh=mesh, in_specs=in_specs, out_specs=out_specs, check_vma=False)
```

```python
import functools
import math

import jax
import jax.numpy as jnp
from jax import lax
from jax.experimental import pallas as pl
from jax.experimental.pallas import tpu as pltpu
from jax.sharding import PartitionSpec as P


HIDDEN = -1e30
TILE = 128
IDROWS = 16
CHUNK = 32
GRANT = 24 * 2**20
F32 = jnp.float32
BF16 = jnp.bfloat16
VM = pl.BlockSpec(memory_space=pltpu.VMEM)
HB = pl.BlockSpec(memory_space=pltpu.HBM)


def passed_on(value, hop):
    count = lax.axis_size("ctx")
    if hop == 1:
        pairs = [(i, (i + 1) % count) for i in range(count)]
    else:
        pairs = [(i, i + 1) for i in range(hop - 1, count - 1)]
    return lax.ppermute(value, "ctx", pairs)


def swapped(value, axis, bit):
    count = lax.axis_size(axis)
    return lax.ppermute(value, axis, [(i, i ^ bit) for i in range(count)])


def one_head_rows(src, first, rows, heads, wide, head):
    if head == 0:
        wide[0 : rows * heads, :] = src[first : first + rows * heads, :].astype(F32)
    return wide[pl.ds(head, rows, stride=heads), :]


def place_keys(src, rows, heads, wide, keys, at):
    for head in range(heads):
        picked = one_head_rows(src, 0, rows, heads, wide, head)
        for j in range(0, rows, TILE):
            keys[head, (at + j) // TILE] = jnp.transpose(picked[j : j + TILE, :]).astype(BF16)


def place_values(src, rows, heads, wide, vals, at):
    for head in range(heads):
        vals[head, at : at + rows, :] = one_head_rows(src, 0, rows, heads, wide, head).astype(BF16)


def id_column(ids, tile):
    return jnp.transpose(jnp.broadcast_to(ids[tile : tile + 1, :].astype(F32), (TILE, TILE)))


def id_row(ids, tile):
    return jnp.broadcast_to(ids[tile : tile + 1, :].astype(F32), (TILE, TILE))


def choose_kernel(kv_local, far_k, far_v, other_k, other_v, out, wide, own_k, own_v, sems):
    moves = [
        pltpu.make_async_copy(far_k, own_k, sems.at[0]),
        pltpu.make_async_copy(far_v, own_v, sems.at[1]),
    ]
    for move in moves:
        move.start()
    for move in moves:
        move.wait()
    positions = out.shape[0] // (4 * kv_local)
    heads = own_k.shape[0] // positions
    start = lax.axis_index("pair") * kv_local
    place = 0
    for mine, other in ((own_k, other_k), (own_v, other_v)):
        for slot, src in enumerate((mine, other)):
            wide[slot] = src[...].astype(F32)
        for head in range(kv_local):
            for slot in range(2):
                picked = wide[slot, pl.ds(start + head, positions, stride=heads), :]
                out[place : place + positions, :] = picked.astype(BF16)
                place += positions


def attend(q, keys, vals, masked, bias, factor, old, keep, emit, scores, peaks, tops, weights):
    qheads, rows, _ = q.shape
    blocks = keys.shape[1]
    group = qheads // keys.shape[0]

    def score(head, slot):
        kv = head // group
        wall = jnp.concatenate([keys[kv, j] for j in range(blocks)], axis=1)
        found = jnp.dot(q[head], wall, preferred_element_type=F32)
        peak = None
        for j in range(blocks):
            piece = found[:, j * TILE : (j + 1) * TILE]
            if j < masked:
                piece = piece + bias[j]
            scores[slot, j] = piece
            peak = piece if peak is None else jnp.maximum(peak, piece)
        peaks[slot] = peak

    def weigh(head, slot):
        for r in range(0, rows, CHUNK):
            part = slice(r, r + CHUNK)
            top = jnp.max(peaks[slot, part, :], axis=1, keepdims=True)
            top = jnp.broadcast_to(top, (CHUNK, TILE))
            if old is not None:
                top = jnp.maximum(top, old[head, part, :])
            if keep is None:
                tops[slot, part, :] = top
            else:
                keep[head, part, :] = top
            for j in range(blocks):
                shifted = (scores[slot, j, part, :] - top) * factor
                weights[slot, j, part, :] = jnp.exp2(shifted).astype(BF16)

    def mix(head, slot):
        wall = jnp.concatenate([weights[slot, j] for j in range(blocks)], axis=1)
        mine = vals[head // group]
        mine = jnp.concatenate([mine, jnp.ones_like(mine)], axis=1)
        mixed = jnp.dot(wall, mine, preferred_element_type=F32)
        emit(head, tops[slot] if keep is None else keep[head], mixed)

    def step(head, slot):
        score(head + 1, 1 - slot)
        weigh(head, slot)
        mix(head - 1, 1 - slot)

    score(0, 0)
    score(1, 1)
    weigh(0, 0)
    trips = (qheads - 2) // 2

    def trip(index, _):
        head = 1 + 2 * index
        step(head, 1)
        step(head + 1, 0)
        return 0

    lax.fori_loop(0, trips, trip, 0)
    for head in range(1 + 2 * trips, qheads - 1):
        step(head, head % 2)
    last = qheads - 1
    weigh(last, last % 2)
    mix(last - 1, (last - 1) % 2)
    mix(last, last % 2)


def absorb_kernel(plan, kv_local, rows, factor, *refs):
    refs = list(refs)
    q, ids = refs.pop(0), refs.pop(0)
    started, final = plan["old"], plan["final"]
    acc = refs.pop(0) if started else None
    stat = refs.pop(0) if started else None
    sources = [(kind, [refs.pop(0) for _ in range(taken)]) for kind, taken in plan["parts"]]
    outs = [refs.pop(0) for _ in range(1 if final else 2)]
    moves = []
    if not started:
        landed, k_here, v_here, sems = refs.pop(0), *refs[-3:]
        refs = refs[:-3]
        (kind, (k_far, v_far)) = sources[0]
        sources[0] = (kind, (k_here, v_here))
        moves = [
            pltpu.make_async_copy(k_far, k_here, sems.at[0]),
            pltpu.make_async_copy(v_far, v_here, sems.at[1]),
            pltpu.make_async_copy(q, landed, sems.at[2]),
        ]
        for move in moves:
            move.start()
        moves[0].wait()
        moves[1].wait()
        q = landed
    keys, vals, wide, bias, *room = refs
    tiles = rows // TILE
    mine = ids[...]
    at = 0
    masked = 0
    for kind, taken in sources:
        if kind == "prefix":
            size = 2 * kv_local * TILE
            for chunk in taken:
                for first in range(0, chunk.shape[0], size):
                    for head in range(kv_local):
                        low = first + head * TILE
                        keys[head, at // TILE] = jnp.transpose(chunk[low : low + TILE, :])
                        low = first + (kv_local + head) * TILE
                        vals[head, at : at + TILE, :] = chunk[low : low + TILE, :]
                    at += TILE
            continue
        place_keys(taken[0], rows, kv_local, wide, keys, at)
        place_values(taken[1], rows, kv_local, wide, vals, at)
        if kind == "own":
            other = mine
            spot = lax.broadcasted_iota(jnp.int32, (TILE, TILE), 0)
            place = lax.broadcasted_iota(jnp.int32, (TILE, TILE), 1)
        else:
            hops = 1 if kind == "back1" else 2
            other = taken[1][rows * kv_local : rows * kv_local + IDROWS, :].astype(F32)
            other = jnp.where(lax.axis_index("ctx") >= hops, other, 0.0)
        for i in range(tiles):
            column = id_column(mine, i)
            part = slice(i * TILE, (i + 1) * TILE)
            for j in range(tiles):
                seen = column == id_row(other, j)
                if kind == "own" and j == i:
                    seen = seen & (place <= spot)
                piece = jnp.where(seen, 0.0, HIDDEN)
                if kind == "own" and j > i:
                    piece = jnp.full((TILE, TILE), HIDDEN, F32)
                bias[at // TILE + j, part, :] = piece
        at += rows
        masked = at // TILE

    def emit(head, top, mixed):
        upper, lower = mixed[:, 0:TILE], mixed[:, TILE:]
        if started:
            fade = jnp.exp2((stat[head] - top) * factor)
            upper = acc[head, :, 0:TILE] * fade + upper
            lower = acc[head, :, TILE:] * fade + lower
        if final:
            outs[0][head] = (upper / lower).astype(BF16)
        else:
            outs[0][head, :, 0:TILE] = upper
            outs[0][head, :, TILE:] = lower

    if not started:
        moves[2].wait()
    keep = None if final else outs[1]
    attend(q, keys, vals, masked, bias, factor, stat, keep, emit, *room)


def absorb(parts, final, queries, ids, state, kv_local, factor):
    qheads, rows, width = queries.shape
    total = 0
    masked = 0
    for kind, arrays in parts:
        total += sum(a.shape[0] for a in arrays) // (2 * kv_local) if kind == "prefix" else rows
        masked = masked if kind == "prefix" else total
    plan = {
        "old": bool(state),
        "final": final,
        "parts": [(kind, len(arrays)) for kind, arrays in parts],
    }
    operands = [queries, ids, *state]
    for kind, arrays in parts:
        operands.extend(arrays)
    if final:
        shape = (jax.ShapeDtypeStruct((qheads, rows, width), BF16),)
    else:
        shape = (
            jax.ShapeDtypeStruct((qheads, rows, 2 * TILE), F32),
            jax.ShapeDtypeStruct((qheads, rows, TILE), F32),
        )
    specs = [VM] * len(operands)
    extra = []
    if not state:
        for at in (0, 2, 3):
            operands[at] = pltpu.with_memory_space_constraint(operands[at], pltpu.HBM)
        specs = [HB, VM, HB, HB] + [VM] * (len(operands) - 4)
        shape += (jax.ShapeDtypeStruct(queries.shape, BF16),)
        block = pltpu.VMEM(parts[0][1][0].shape, BF16)
        extra = [block, block, pltpu.SemaphoreType.DMA((3,))]
    return pl.pallas_call(
        functools.partial(absorb_kernel, plan, kv_local, rows, factor),
        out_shape=shape,
        in_specs=specs,
        out_specs=(VM,) * len(shape),
        scratch_shapes=[
            pltpu.VMEM((kv_local, total // TILE, width, TILE), BF16),
            pltpu.VMEM((kv_local, total, width), BF16),
            pltpu.VMEM((rows * kv_local, width), F32),
            pltpu.VMEM((max(masked, TILE) // TILE, rows, TILE), F32),
            *working_room(rows, total),
            *extra,
        ],
        cost_estimate=pl.CostEstimate(
            flops=4 * rows * qheads * total * width,
            bytes_accessed=4 * 2**20,
            transcendentals=rows * qheads * total,
        ),
        compiler_params=pltpu.CompilerParams(vmem_limit_bytes=GRANT),
    )(*operands)


def working_room(rows, total):
    return [
        pltpu.VMEM((2, total // TILE, rows, TILE), F32),
        pltpu.VMEM((2, rows, TILE), F32),
        pltpu.VMEM((2, rows, TILE), F32),
        pltpu.VMEM((2, total // TILE, rows, TILE), BF16),
    ]


def shards(query_suffix, key_suffix, value_suffix, key_prefix, value_prefix, file_ids):
    rows, _, width = query_suffix.shape
    kv_local = key_suffix.shape[1]
    factor = math.log2(math.e) / math.sqrt(width)
    count = lax.axis_size("ctx")
    queries = query_suffix.transpose(1, 0, 2)
    k0 = key_suffix.reshape(rows * kv_local, width)
    v0 = value_suffix.reshape(rows * kv_local, width)
    ids = (file_ids + 1).astype(BF16).reshape(rows // TILE, TILE)
    ids = jnp.pad(ids, ((0, IDROWS - rows // TILE), (0, 0)))
    k1 = passed_on(k0, 1)
    v1 = passed_on(jnp.concatenate([v0, ids]), 1)
    kp = key_prefix.reshape(-1, width)
    vp = value_prefix.reshape(-1, width)
    kp_other = swapped(kp, "pair", 1)
    vp_other = swapped(vp, "pair", 1)
    positions = key_prefix.shape[0]
    mine = pl.pallas_call(
        functools.partial(choose_kernel, kv_local),
        out_shape=jax.ShapeDtypeStruct((4 * kv_local * positions, width), BF16),
        in_specs=[HB, HB, VM, VM],
        out_specs=VM,
        scratch_shapes=[
            pltpu.VMEM((2,) + kp.shape, F32),
            pltpu.VMEM(kp.shape, BF16),
            pltpu.VMEM(vp.shape, BF16),
            pltpu.SemaphoreType.DMA((2,)),
        ],
        cost_estimate=pl.CostEstimate(flops=0, bytes_accessed=4 * kp.size * 2, transcendentals=0),
        compiler_params=pltpu.CompilerParams(vmem_limit_bytes=GRANT),
        name="choose",
    )(
        pltpu.with_memory_space_constraint(kp, pltpu.HBM),
        pltpu.with_memory_space_constraint(vp, pltpu.HBM),
        kp_other,
        vp_other,
    )
    k2 = passed_on(k1, 2)
    v2 = passed_on(v1, 2)
    prefix = [mine]
    bit = 1
    while bit < count:
        whole = jnp.concatenate(prefix) if len(prefix) > 1 else mine
        prefix.append(swapped(whole, "ctx", bit))
        bit *= 2
    rest = (kv_local, factor)
    early = [("own", [k0, v0]), ("back1", [k1, v1])]
    *state, queries = absorb(early, False, queries, ids, (), *rest)
    args = (queries, ids)
    late = [("back2", [k2, v2]), ("prefix", prefix[:-1])]
    state = absorb(late, False, *args, state, *rest)
    (out,) = absorb([("prefix", prefix[-1:])], True, *args, state, *rest)
    return out.transpose(1, 0, 2)


def solution(mesh):
    in_specs = (
        P(("groups", "ctx"), ("head", "pair"), None),
        P(("groups", "ctx"), ("head", "pair"), None),
        P(("groups", "ctx"), ("head", "pair"), None),
        P(("groups", "ctx", "pair"), "head", None),
        P(("groups", "ctx", "pair"), "head", None),
        P(("groups", "ctx")),
    )
    out_specs = P(("groups", "ctx"), ("head", "pair"), None)

    return jax.shard_map(shards, mesh=mesh, in_specs=in_specs, out_specs=out_specs, check_vma=False)
```

```python
import functools
import math

import jax
import jax.numpy as jnp
from jax import lax
from jax.experimental import pallas as pl
from jax.experimental.pallas import tpu as pltpu
from jax.sharding import PartitionSpec as P


HIDDEN = -1e30
TILE = 128
IDROWS = 16
CHUNK = 32
UNROLL = 4
GRANT = 24 * 2**20
F32 = jnp.float32
BF16 = jnp.bfloat16
VM = pl.BlockSpec(memory_space=pltpu.VMEM)
HB = pl.BlockSpec(memory_space=pltpu.HBM)


def passed_on(value, hop):
    count = lax.axis_size("ctx")
    if hop == 1:
        pairs = [(i, (i + 1) % count) for i in range(count)]
    else:
        pairs = [(i, i + 1) for i in range(hop - 1, count - 1)]
    return lax.ppermute(value, "ctx", pairs)


def swapped(value, axis, bit):
    count = lax.axis_size(axis)
    return lax.ppermute(value, axis, [(i, i ^ bit) for i in range(count)])


def one_head_rows(src, first, rows, heads, wide, head):
    if head == 0:
        wide[0 : rows * heads, :] = src[first : first + rows * heads, :].astype(F32)
    return wide[pl.ds(head, rows, stride=heads), :]


def place_keys(src, rows, heads, wide, keys, at):
    for head in range(heads):
        picked = one_head_rows(src, 0, rows, heads, wide, head)
        for j in range(0, rows, TILE):
            keys[head, (at + j) // TILE] = jnp.transpose(picked[j : j + TILE, :].astype(BF16))


def place_values(src, rows, heads, wide, vals, at):
    for head in range(heads):
        vals[head, at : at + rows, :] = one_head_rows(src, 0, rows, heads, wide, head).astype(BF16)


def id_column(ids, tile):
    return jnp.transpose(jnp.broadcast_to(ids[tile : tile + 1, :].astype(F32), (TILE, TILE)))


def id_row(ids, tile):
    return jnp.broadcast_to(ids[tile : tile + 1, :].astype(F32), (TILE, TILE))


def choose_kernel(kv_local, far_k, far_v, other_k, other_v, out, wide, own_k, own_v, sems):
    moves = [
        pltpu.make_async_copy(far_k, own_k, sems.at[0]),
        pltpu.make_async_copy(far_v, own_v, sems.at[1]),
    ]
    for move in moves:
        move.start()
    for move in moves:
        move.wait()
    positions = out.shape[0] // (4 * kv_local)
    heads = own_k.shape[0] // positions
    start = lax.axis_index("pair") * kv_local
    place = 0
    for mine, other in ((own_k, other_k), (own_v, other_v)):
        for slot, src in enumerate((mine, other)):
            wide[slot] = src[...].astype(F32)
        for head in range(kv_local):
            for slot in range(2):
                picked = wide[slot, pl.ds(start + head, positions, stride=heads), :]
                out[place : place + positions, :] = picked.astype(BF16)
                place += positions


def attend(q, keys, vals, masked, bias, factor, old, keep, emit, scores, peaks, tops, weights):
    qheads, rows, _ = q.shape
    blocks = keys.shape[1]
    group = qheads // keys.shape[0]

    def score(head, slot):
        kv = head // group
        wall = jnp.concatenate([keys[kv, j] for j in range(blocks)], axis=1)
        found = jnp.dot(q[head], wall, preferred_element_type=F32)
        peak = None
        for j in range(blocks):
            piece = found[:, j * TILE : (j + 1) * TILE]
            if j < masked:
                piece = piece + bias[j]
            scores[slot, j] = piece
            peak = piece if peak is None else jnp.maximum(peak, piece)
        peaks[slot] = peak

    def weigh(head, slot):
        for r in range(0, rows, CHUNK):
            part = slice(r, r + CHUNK)
            top = jnp.max(peaks[slot, part, :], axis=1, keepdims=True)
            top = jnp.broadcast_to(top, (CHUNK, TILE))
            if old is not None:
                top = jnp.maximum(top, old[head, part, :])
            if keep is None:
                tops[slot, part, :] = top
            else:
                keep[head, part, :] = top
            for j in range(blocks):
                shifted = (scores[slot, j, part, :] - top) * factor
                weights[slot, j, part, :] = jnp.exp2(shifted).astype(BF16)

    def mix(head, slot):
        wall = jnp.concatenate([weights[slot, j] for j in range(blocks)], axis=1)
        mine = vals[head // group]
        mine = jnp.concatenate([mine, jnp.ones_like(mine)], axis=1)
        mixed = jnp.dot(wall, mine, preferred_element_type=F32)
        emit(head, tops[slot] if keep is None else keep[head], mixed)

    def step(head, slot):
        score(head + 1, 1 - slot)
        weigh(head, slot)
        mix(head - 1, 1 - slot)

    score(0, 0)
    score(1, 1)
    weigh(0, 0)
    trips = (qheads - 2) // UNROLL

    def trip(index, _):
        for ahead in range(1, UNROLL + 1):
            step(UNROLL * index + ahead, ahead % 2)
        return 0

    lax.fori_loop(0, trips, trip, 0)
    for head in range(1 + UNROLL * trips, qheads - 1):
        step(head, head % 2)
    last = qheads - 1
    weigh(last, last % 2)
    mix(last - 1, (last - 1) % 2)
    mix(last, last % 2)


def absorb_kernel(plan, kv_local, rows, factor, *refs):
    refs = list(refs)
    q, ids = refs.pop(0), refs.pop(0)
    started, final = plan["old"], plan["final"]
    acc = refs.pop(0) if started else None
    stat = refs.pop(0) if started else None
    sources = [(kind, [refs.pop(0) for _ in range(taken)]) for kind, taken in plan["parts"]]
    outs = [refs.pop(0) for _ in range(1 if final else 2)]
    moves = []
    if not started:
        landed, k_here, v_here, sems = refs.pop(0), *refs[-3:]
        refs = refs[:-3]
        (kind, (k_far, v_far)) = sources[0]
        sources[0] = (kind, (k_here, v_here))
        moves = [
            pltpu.make_async_copy(k_far, k_here, sems.at[0]),
            pltpu.make_async_copy(v_far, v_here, sems.at[1]),
            pltpu.make_async_copy(q, landed, sems.at[2]),
        ]
        for move in moves:
            move.start()
        q = landed
    if plan["skips"]:
        acc, stat = outs
    if final:
        ready, leaving = refs[-2:]
        refs = refs[:-2]
    keys, vals, wide, bias, *room = refs

    def visible_at_all():
        source = sources[0][1][1]
        last = source[rows * kv_local : rows * kv_local + IDROWS, :].astype(F32)
        apart = last[rows // TILE - 1 : rows // TILE, TILE - 1 :] - ids[...].astype(F32)[0:1, 0:1]
        return (lax.axis_index("ctx") >= 2) & (jnp.max(jnp.abs(apart)) < 0.5)

    def work():
        tiles = rows // TILE
        mine = ids[...]
        at = 0
        masked = 0
        places = []
        for kind, taken in sources:
            places.append((kind == "own", at, kind, taken))
            if kind == "prefix":
                at += sum(chunk.shape[0] for chunk in taken) // (2 * kv_local)
            else:
                at += rows
                masked = at // TILE
        for own, at, kind, taken in sorted(places, key=lambda place: place[:2]):
            if kind == "prefix":
                size = 2 * kv_local * TILE
                for chunk in taken:
                    for first in range(0, chunk.shape[0], size):
                        for head in range(kv_local):
                            low = first + head * TILE
                            keys[head, at // TILE] = jnp.transpose(chunk[low : low + TILE, :])
                            low = first + (kv_local + head) * TILE
                            vals[head, at : at + TILE, :] = chunk[low : low + TILE, :]
                        at += TILE
                continue
            if kind == "own":
                other = mine
                spot = lax.broadcasted_iota(jnp.int32, (TILE, TILE), 0)
                place = lax.broadcasted_iota(jnp.int32, (TILE, TILE), 1)
            else:
                hops = 1 if kind == "back1" else 2
                other = taken[1][rows * kv_local : rows * kv_local + IDROWS, :].astype(F32)
                other = jnp.where(lax.axis_index("ctx") >= hops, other, 0.0)
            for i in range(tiles):
                column = id_column(mine, i)
                part = slice(i * TILE, (i + 1) * TILE)
                for j in range(tiles):
                    seen = column == id_row(other, j)
                    if kind == "own" and j == i:
                        seen = seen & (place <= spot)
                    piece = jnp.where(seen, 0.0, HIDDEN)
                    if kind == "own" and j > i:
                        piece = jnp.full((TILE, TILE), HIDDEN, F32)
                    bias[at // TILE + j, part, :] = piece
            if own:
                moves[0].wait()
                moves[1].wait()
            place_keys(taken[0], rows, kv_local, wide, keys, at)
            place_values(taken[1], rows, kv_local, wide, vals, at)

        def emit(head, top, mixed):
            upper, lower = mixed[:, 0:TILE], mixed[:, TILE:]
            if started:
                fade = jnp.exp2((stat[head] - top) * factor)
                upper = acc[head, :, 0:TILE] * fade + upper
                lower = acc[head, :, TILE:] * fade + lower
            if final:
                ready[head] = (upper / lower).astype(BF16)
                pltpu.make_async_copy(ready.at[head], outs[0].at[head], leaving.at[head]).start()
            else:
                outs[0][head, :, 0:TILE] = upper
                outs[0][head, :, TILE:] = lower
                if started:
                    outs[1][head] = top

        if not started:
            moves[2].wait()
        keep = None if final or plan["skips"] else outs[1]
        attend(q, keys, vals, masked, bias, factor, stat, keep, emit, *room)

    if plan["skips"]:
        pl.when(visible_at_all())(work)
    else:
        work()
    if final:
        for head in range(q.shape[0]):
            pltpu.make_async_copy(ready.at[head], outs[0].at[head], leaving.at[head]).wait()


def absorb(parts, final, queries, ids, state, kv_local, factor):
    qheads, rows, width = queries.shape
    total = 0
    masked = 0
    for kind, arrays in parts:
        total += sum(a.shape[0] for a in arrays) // (2 * kv_local) if kind == "prefix" else rows
        masked = masked if kind == "prefix" else total
    plan = {
        "old": bool(state),
        "final": final,
        "skips": [kind for kind, _ in parts] == ["back2"] and not final,
        "parts": [(kind, len(arrays)) for kind, arrays in parts],
    }
    operands = [queries, ids, *state]
    for kind, arrays in parts:
        operands.extend(arrays)
    if final:
        shape = (jax.ShapeDtypeStruct((qheads, rows, width), BF16),)
    else:
        shape = (
            jax.ShapeDtypeStruct((qheads, rows, 2 * TILE), F32),
            jax.ShapeDtypeStruct((qheads, rows, TILE), F32),
        )
    specs = [VM] * len(operands)
    extra = []
    if not state:
        for at in (0, 2, 3):
            operands[at] = pltpu.with_memory_space_constraint(operands[at], pltpu.HBM)
        specs = [HB, VM, HB, HB] + [VM] * (len(operands) - 4)
        shape += (jax.ShapeDtypeStruct(queries.shape, BF16),)
        block = pltpu.VMEM(parts[0][1][0].shape, BF16)
        extra = [block, block, pltpu.SemaphoreType.DMA((3,))]
    out_specs = (VM,) * len(shape)
    aliases = {}
    if final:
        out_specs = (HB,)
        extra = [pltpu.VMEM(shape[0].shape, BF16), pltpu.SemaphoreType.DMA((qheads,))]
    elif plan["skips"]:
        aliases = {2: 0, 3: 1}
    return pl.pallas_call(
        functools.partial(absorb_kernel, plan, kv_local, rows, factor),
        out_shape=shape,
        in_specs=specs,
        out_specs=out_specs,
        input_output_aliases=aliases,
        scratch_shapes=[
            pltpu.VMEM((kv_local, total // TILE, width, TILE), BF16),
            pltpu.VMEM((kv_local, total, width), BF16),
            pltpu.VMEM((rows * kv_local, width), F32),
            pltpu.VMEM((max(masked, TILE) // TILE, rows, TILE), F32),
            *working_room(rows, total),
            *extra,
        ],
        cost_estimate=pl.CostEstimate(
            flops=4 * rows * qheads * total * width,
            bytes_accessed=4 * 2**20,
            transcendentals=rows * qheads * total,
        ),
        compiler_params=pltpu.CompilerParams(vmem_limit_bytes=GRANT),
    )(*operands)


def working_room(rows, total):
    return [
        pltpu.VMEM((2, total // TILE, rows, TILE), F32),
        pltpu.VMEM((2, rows, TILE), F32),
        pltpu.VMEM((2, rows, TILE), F32),
        pltpu.VMEM((2, total // TILE, rows, TILE), BF16),
    ]


def shards(query_suffix, key_suffix, value_suffix, key_prefix, value_prefix, file_ids):
    rows, _, width = query_suffix.shape
    kv_local = key_suffix.shape[1]
    factor = math.log2(math.e) / math.sqrt(width)
    count = lax.axis_size("ctx")
    queries = query_suffix.transpose(1, 0, 2)
    k0 = key_suffix.reshape(rows * kv_local, width)
    v0 = value_suffix.reshape(rows * kv_local, width)
    ids = (file_ids + 1).astype(BF16).reshape(rows // TILE, TILE)
    ids = jnp.pad(ids, ((0, IDROWS - rows // TILE), (0, 0)))
    k1 = passed_on(k0, 1)
    v1 = passed_on(jnp.concatenate([v0, ids]), 1)
    kp = key_prefix.reshape(-1, width)
    vp = value_prefix.reshape(-1, width)
    kp_other = swapped(kp, "pair", 1)
    vp_other = swapped(vp, "pair", 1)
    positions = key_prefix.shape[0]
    mine = pl.pallas_call(
        functools.partial(choose_kernel, kv_local),
        out_shape=jax.ShapeDtypeStruct((4 * kv_local * positions, width), BF16),
        in_specs=[HB, HB, VM, VM],
        out_specs=VM,
        scratch_shapes=[
            pltpu.VMEM((2,) + kp.shape, F32),
            pltpu.VMEM(kp.shape, BF16),
            pltpu.VMEM(vp.shape, BF16),
            pltpu.SemaphoreType.DMA((2,)),
        ],
        cost_estimate=pl.CostEstimate(flops=0, bytes_accessed=4 * kp.size * 2, transcendentals=0),
        compiler_params=pltpu.CompilerParams(vmem_limit_bytes=GRANT),
        name="choose",
    )(
        pltpu.with_memory_space_constraint(kp, pltpu.HBM),
        pltpu.with_memory_space_constraint(vp, pltpu.HBM),
        kp_other,
        vp_other,
    )
    k2 = passed_on(k1, 2)
    v2 = passed_on(v1, 2)
    prefix = [mine]
    bit = count // 2
    while bit:
        whole = jnp.concatenate(prefix) if len(prefix) > 1 else mine
        prefix.append(swapped(whole, "ctx", bit))
        bit //= 2
    rest = (kv_local, factor)
    *state, queries = absorb([("own", [k0, v0])], False, queries, ids, (), *rest)
    args = (queries, ids)
    near = [("back1", [k1, v1]), ("prefix", prefix[:-1])]
    state = absorb(near, False, *args, state, *rest)
    state = absorb([("back2", [k2, v2])], False, *args, state, *rest)
    (out,) = absorb([("prefix", prefix[-1:])], True, *args, state, *rest)
    return out.transpose(1, 0, 2)


def solution(mesh):
    in_specs = (
        P(("groups", "ctx"), ("head", "pair"), None),
        P(("groups", "ctx"), ("head", "pair"), None),
        P(("groups", "ctx"), ("head", "pair"), None),
        P(("groups", "ctx", "pair"), "head", None),
        P(("groups", "ctx", "pair"), "head", None),
        P(("groups", "ctx")),
    )
    out_specs = P(("groups", "ctx"), ("head", "pair"), None)

    return jax.shard_map(shards, mesh=mesh, in_specs=in_specs, out_specs=out_specs, check_vma=False)
```

```python
import functools
import math

import jax
import jax.numpy as jnp
from jax import lax
from jax.experimental import pallas as pl
from jax.experimental.pallas import tpu as pltpu
from jax.sharding import PartitionSpec as P


HIDDEN = -1e30
TILE = 128
IDROWS = 16
CHUNK = 32
GRANT = 24 * 2**20
F32 = jnp.float32
BF16 = jnp.bfloat16
VM = pl.BlockSpec(memory_space=pltpu.VMEM)
HB = pl.BlockSpec(memory_space=pltpu.HBM)


def passed_on(value, hop):
    count = lax.axis_size("ctx")
    if hop == 1:
        pairs = [(i, (i + 1) % count) for i in range(count)]
    else:
        pairs = [(i, i + 1) for i in range(hop - 1, count - 1)]
    return lax.ppermute(value, "ctx", pairs)


def swapped(value, axis, bit):
    count = lax.axis_size(axis)
    return lax.ppermute(value, axis, [(i, i ^ bit) for i in range(count)])


def one_head_rows(src, first, rows, heads, wide, head):
    if head == 0:
        wide[0 : rows * heads, :] = src[first : first + rows * heads, :].astype(F32)
    return wide[pl.ds(head, rows, stride=heads), :]


def place_keys(src, rows, heads, wide, keys, at):
    for head in range(heads):
        picked = one_head_rows(src, 0, rows, heads, wide, head)
        for j in range(0, rows, TILE):
            keys[head, (at + j) // TILE] = jnp.transpose(picked[j : j + TILE, :].astype(BF16))


def place_values(src, rows, heads, wide, vals, at):
    for head in range(heads):
        vals[head, at : at + rows, :] = one_head_rows(src, 0, rows, heads, wide, head).astype(BF16)


def id_column(ids, tile):
    return jnp.transpose(jnp.broadcast_to(ids[tile : tile + 1, :].astype(F32), (TILE, TILE)))


def id_row(ids, tile):
    return jnp.broadcast_to(ids[tile : tile + 1, :].astype(F32), (TILE, TILE))


def choose_kernel(kv_local, far_k, far_v, other_k, other_v, out, wide, own_k, own_v, sems):
    moves = [
        pltpu.make_async_copy(far_k, own_k, sems.at[0]),
        pltpu.make_async_copy(far_v, own_v, sems.at[1]),
    ]
    for move in moves:
        move.start()
    for move in moves:
        move.wait()
    positions = out.shape[0] // (4 * kv_local)
    heads = own_k.shape[0] // positions
    start = lax.axis_index("pair") * kv_local
    place = 0
    for mine, other in ((own_k, other_k), (own_v, other_v)):
        for slot, src in enumerate((mine, other)):
            wide[slot] = src[...].astype(F32)
        for head in range(kv_local):
            halves = [
                wide[slot, pl.ds(start + head, positions, stride=heads), :].astype(BF16)
                for slot in range(2)
            ]
            tile = jnp.concatenate(halves, axis=0)
            if mine is own_k:
                tile = jnp.transpose(tile)
            out[place : place + TILE, :] = tile
            place += TILE


def attend(
    q, keys, vals, masked, bias, factor, old, keep, emit, unroll, scores, peaks, tops, weights
):
    qheads, rows, _ = q.shape
    blocks = keys.shape[1]
    group = qheads // keys.shape[0]

    def score(head, slot):
        kv = head // group
        wall = jnp.concatenate([keys[kv, j] for j in range(blocks)], axis=1)
        found = jnp.dot(q[head], wall, preferred_element_type=F32)
        peak = None
        for j in range(blocks):
            piece = found[:, j * TILE : (j + 1) * TILE]
            if j < masked:
                piece = piece + bias[j]
            scores[slot, j] = piece
            peak = piece if peak is None else jnp.maximum(peak, piece)
        peaks[slot] = peak

    def weigh(head, slot):
        for r in range(0, rows, CHUNK):
            part = slice(r, r + CHUNK)
            top = jnp.max(peaks[slot, part, :], axis=1, keepdims=True)
            top = jnp.broadcast_to(top, (CHUNK, TILE))
            if old is not None:
                top = jnp.maximum(top, old[head, part, :])
            if keep is None:
                tops[slot, part, :] = top
            else:
                keep[head, part, :] = top
            for j in range(blocks):
                shifted = (scores[slot, j, part, :] - top) * factor
                weights[slot, j, part, :] = jnp.exp2(shifted).astype(BF16)

    def mix(head, slot):
        wall = jnp.concatenate([weights[slot, j] for j in range(blocks)], axis=1)
        mine = vals[head // group]
        mine = jnp.concatenate([mine, jnp.ones_like(mine)], axis=1)
        mixed = jnp.dot(wall, mine, preferred_element_type=F32)
        emit(head, tops[slot] if keep is None else keep[head], mixed)

    def step(head, slot):
        score(head + 1, 1 - slot)
        weigh(head, slot)
        mix(head - 1, 1 - slot)

    score(0, 0)
    score(1, 1)
    weigh(0, 0)
    trips = (qheads - 2) // unroll

    def trip(index, _):
        for ahead in range(1, unroll + 1):
            step(unroll * index + ahead, ahead % 2)
        return 0

    lax.fori_loop(0, trips, trip, 0)
    for head in range(1 + unroll * trips, qheads - 1):
        step(head, head % 2)
    last = qheads - 1
    weigh(last, last % 2)
    mix(last - 1, (last - 1) % 2)
    mix(last, last % 2)


def absorb_kernel(plan, kv_local, rows, factor, *refs):
    refs = list(refs)
    q, ids = refs.pop(0), refs.pop(0)
    started, final = plan["old"], plan["final"]
    acc = refs.pop(0) if started else None
    stat = refs.pop(0) if started else None
    sources = [(kind, [refs.pop(0) for _ in range(taken)]) for kind, taken in plan["parts"]]
    outs = [refs.pop(0) for _ in range(1 if final else 2)]
    moves = []
    if not started:
        landed, k_here, v_here, sems = refs.pop(0), *refs[-3:]
        refs = refs[:-3]
        (kind, (k_far, v_far)) = sources[0]
        sources[0] = (kind, (k_here, v_here))
        moves = [
            pltpu.make_async_copy(k_far, k_here, sems.at[0]),
            pltpu.make_async_copy(v_far, v_here, sems.at[1]),
            pltpu.make_async_copy(q, landed, sems.at[2]),
        ]
        for move in moves:
            move.start()
        q = landed
    if plan["skips"]:
        acc, stat = outs
    if final:
        ready, leaving = refs[-2:]
        refs = refs[:-2]
    keys, vals, wide, bias, *room = refs

    def visible_at_all():
        source = sources[0][1][1]
        last = source[rows * kv_local : rows * kv_local + IDROWS, :].astype(F32)
        apart = last[rows // TILE - 1 : rows // TILE, TILE - 1 :] - ids[...].astype(F32)[0:1, 0:1]
        return (lax.axis_index("ctx") >= 2) & (jnp.max(jnp.abs(apart)) < 0.5)

    def work():
        tiles = rows // TILE
        mine = ids[...]
        at = 0
        masked = 0
        places = []
        for kind, taken in sources:
            places.append((kind == "own", at, kind, taken))
            if kind == "prefix":
                at += sum(chunk.shape[0] for chunk in taken) // (2 * kv_local)
            else:
                at += rows
                masked = at // TILE
        for own, at, kind, taken in sorted(places, key=lambda place: place[:2]):
            if kind == "prefix":
                size = 2 * kv_local * TILE
                for chunk in taken:
                    for first in range(0, chunk.shape[0], size):
                        for head in range(kv_local):
                            low = first + head * TILE
                            keys[head, at // TILE] = chunk[low : low + TILE, :]
                            low = first + (kv_local + head) * TILE
                            vals[head, at : at + TILE, :] = chunk[low : low + TILE, :]
                        at += TILE
                continue
            if kind == "own":
                other = mine
                spot = lax.broadcasted_iota(jnp.int32, (TILE, TILE), 0)
                place = lax.broadcasted_iota(jnp.int32, (TILE, TILE), 1)
            else:
                hops = 1 if kind == "back1" else 2
                other = taken[1][rows * kv_local : rows * kv_local + IDROWS, :].astype(F32)
                other = jnp.where(lax.axis_index("ctx") >= hops, other, 0.0)
            for i in range(tiles):
                column = id_column(mine, i)
                part = slice(i * TILE, (i + 1) * TILE)
                for j in range(tiles):
                    seen = column == id_row(other, j)
                    if kind == "own" and j == i:
                        seen = seen & (place <= spot)
                    piece = jnp.where(seen, 0.0, HIDDEN)
                    if kind == "own" and j > i:
                        piece = jnp.full((TILE, TILE), HIDDEN, F32)
                    bias[at // TILE + j, part, :] = piece
            if own:
                moves[0].wait()
                moves[1].wait()
            place_keys(taken[0], rows, kv_local, wide, keys, at)
            place_values(taken[1], rows, kv_local, wide, vals, at)

        def emit(head, top, mixed):
            upper, lower = mixed[:, 0:TILE], mixed[:, TILE:]
            if started:
                fade = jnp.exp2((stat[head] - top) * factor)
                upper = acc[head, :, 0:TILE] * fade + upper
                lower = acc[head, :, TILE:] * fade + lower
            if final:
                ready[head] = (upper / lower).astype(BF16)
                pltpu.make_async_copy(ready.at[head], outs[0].at[head], leaving.at[head]).start()
            else:
                outs[0][head, :, 0:TILE] = upper
                outs[0][head, :, TILE:] = lower
                if started:
                    outs[1][head] = top

        if not started:
            moves[2].wait()
        keep = None if final or plan["skips"] else outs[1]
        attend(q, keys, vals, masked, bias, factor, stat, keep, emit, 8 if final else 4, *room)

    if plan["skips"]:
        pl.when(visible_at_all())(work)
    else:
        work()
    if final:
        for head in range(q.shape[0]):
            pltpu.make_async_copy(ready.at[head], outs[0].at[head], leaving.at[head]).wait()


def absorb(parts, final, queries, ids, state, kv_local, factor):
    qheads, rows, width = queries.shape
    total = 0
    masked = 0
    for kind, arrays in parts:
        total += sum(a.shape[0] for a in arrays) // (2 * kv_local) if kind == "prefix" else rows
        masked = masked if kind == "prefix" else total
    plan = {
        "old": bool(state),
        "final": final,
        "skips": [kind for kind, _ in parts] == ["back2"] and not final,
        "parts": [(kind, len(arrays)) for kind, arrays in parts],
    }
    operands = [queries, ids, *state]
    for kind, arrays in parts:
        operands.extend(arrays)
    if final:
        shape = (jax.ShapeDtypeStruct((qheads, rows, width), BF16),)
    else:
        shape = (
            jax.ShapeDtypeStruct((qheads, rows, 2 * TILE), F32),
            jax.ShapeDtypeStruct((qheads, rows, TILE), F32),
        )
    specs = [VM] * len(operands)
    extra = []
    if not state:
        for at in (0, 2, 3):
            operands[at] = pltpu.with_memory_space_constraint(operands[at], pltpu.HBM)
        specs = [HB, VM, HB, HB] + [VM] * (len(operands) - 4)
        shape += (jax.ShapeDtypeStruct(queries.shape, BF16),)
        block = pltpu.VMEM(parts[0][1][0].shape, BF16)
        extra = [block, block, pltpu.SemaphoreType.DMA((3,))]
    out_specs = (VM,) * len(shape)
    aliases = {}
    if final:
        out_specs = (HB,)
        extra = [pltpu.VMEM(shape[0].shape, BF16), pltpu.SemaphoreType.DMA((qheads,))]
    elif plan["skips"]:
        aliases = {2: 0, 3: 1}
    return pl.pallas_call(
        functools.partial(absorb_kernel, plan, kv_local, rows, factor),
        out_shape=shape,
        in_specs=specs,
        out_specs=out_specs,
        input_output_aliases=aliases,
        scratch_shapes=[
            pltpu.VMEM((kv_local, total // TILE, width, TILE), BF16),
            pltpu.VMEM((kv_local, total, width), BF16),
            pltpu.VMEM((rows * kv_local, width), F32),
            pltpu.VMEM((max(masked, TILE) // TILE, rows, TILE), F32),
            *working_room(rows, total),
            *extra,
        ],
        cost_estimate=pl.CostEstimate(
            flops=4 * rows * qheads * total * width,
            bytes_accessed=4 * 2**20,
            transcendentals=rows * qheads * total,
        ),
        compiler_params=pltpu.CompilerParams(vmem_limit_bytes=GRANT),
    )(*operands)


def working_room(rows, total):
    return [
        pltpu.VMEM((2, total // TILE, rows, TILE), F32),
        pltpu.VMEM((2, rows, TILE), F32),
        pltpu.VMEM((2, rows, TILE), F32),
        pltpu.VMEM((2, total // TILE, rows, TILE), BF16),
    ]


def shards(query_suffix, key_suffix, value_suffix, key_prefix, value_prefix, file_ids):
    rows, _, width = query_suffix.shape
    kv_local = key_suffix.shape[1]
    factor = math.log2(math.e) / math.sqrt(width)
    count = lax.axis_size("ctx")
    queries = query_suffix.transpose(1, 0, 2)
    k0 = key_suffix.reshape(rows * kv_local, width)
    v0 = value_suffix.reshape(rows * kv_local, width)
    ids = (file_ids + 1).astype(BF16).reshape(rows // TILE, TILE)
    ids = jnp.pad(ids, ((0, IDROWS - rows // TILE), (0, 0)))
    k1 = passed_on(k0, 1)
    v1 = passed_on(jnp.concatenate([v0, ids]), 1)
    kp = key_prefix.reshape(-1, width)
    vp = value_prefix.reshape(-1, width)
    kp_other = swapped(kp, "pair", 1)
    vp_other = swapped(vp, "pair", 1)
    positions = key_prefix.shape[0]
    mine = pl.pallas_call(
        functools.partial(choose_kernel, kv_local),
        out_shape=jax.ShapeDtypeStruct((4 * kv_local * positions, width), BF16),
        in_specs=[HB, HB, VM, VM],
        out_specs=VM,
        scratch_shapes=[
            pltpu.VMEM((2,) + kp.shape, F32),
            pltpu.VMEM(kp.shape, BF16),
            pltpu.VMEM(vp.shape, BF16),
            pltpu.SemaphoreType.DMA((2,)),
        ],
        cost_estimate=pl.CostEstimate(flops=0, bytes_accessed=4 * kp.size * 2, transcendentals=0),
        compiler_params=pltpu.CompilerParams(vmem_limit_bytes=GRANT),
        name="choose",
    )(
        pltpu.with_memory_space_constraint(kp, pltpu.HBM),
        pltpu.with_memory_space_constraint(vp, pltpu.HBM),
        kp_other,
        vp_other,
    )
    k2 = passed_on(k1, 2)
    v2 = passed_on(v1, 2)
    prefix, arrived = [mine], []
    bit = count // 2
    while bit:
        groups = [prefix[:1], prefix[1:]] if bit == 1 else [prefix]
        for group in groups:
            whole = jnp.concatenate(group) if len(group) > 1 else group[0]
            arrived.append(swapped(whole, "ctx", bit))
        prefix = prefix + arrived
        arrived = []
        bit //= 2
    rest = (kv_local, factor)
    *state, queries = absorb([("own", [k0, v0])], False, queries, ids, (), *rest)
    args = (queries, ids)
    near = [("back1", [k1, v1]), ("prefix", prefix[:-1])]
    state = absorb(near, False, *args, state, *rest)
    state = absorb([("back2", [k2, v2])], False, *args, state, *rest)
    (out,) = absorb([("prefix", prefix[-1:])], True, *args, state, *rest)
    return out.transpose(1, 0, 2)


def solution(mesh):
    in_specs = (
        P(("groups", "ctx"), ("head", "pair"), None),
        P(("groups", "ctx"), ("head", "pair"), None),
        P(("groups", "ctx"), ("head", "pair"), None),
        P(("groups", "ctx", "pair"), "head", None),
        P(("groups", "ctx", "pair"), "head", None),
        P(("groups", "ctx")),
    )
    out_specs = P(("groups", "ctx"), ("head", "pair"), None)

    return jax.shard_map(shards, mesh=mesh, in_specs=in_specs, out_specs=out_specs, check_vma=False)
```

```python
import functools
import math

import jax
import jax.numpy as jnp
from jax import lax
from jax.experimental import pallas as pl
from jax.experimental.pallas import tpu as pltpu
from jax.sharding import PartitionSpec as P


HIDDEN = -1e30
TILE = 128
IDROWS = 16
CHUNK = 32
GRANT = 24 * 2**20
F32 = jnp.float32
BF16 = jnp.bfloat16
VM = pl.BlockSpec(memory_space=pltpu.VMEM)
HB = pl.BlockSpec(memory_space=pltpu.HBM)


def passed_on(value, hop):
    count = lax.axis_size("ctx")
    if hop == 1:
        pairs = [(i, (i + 1) % count) for i in range(count)]
    else:
        pairs = [(i, i + 1) for i in range(hop - 1, count - 1)]
    return lax.ppermute(value, "ctx", pairs)


def swapped(value, axis, bit):
    count = lax.axis_size(axis)
    return lax.ppermute(value, axis, [(i, i ^ bit) for i in range(count)])


def one_head_rows(src, first, rows, heads, wide, head):
    if head == 0:
        wide[0 : rows * heads, :] = src[first : first + rows * heads, :].astype(F32)
    return wide[pl.ds(head, rows, stride=heads), :]


def place_keys(src, rows, heads, wide, keys, at):
    for head in range(heads):
        picked = one_head_rows(src, 0, rows, heads, wide, head)
        for j in range(0, rows, TILE):
            keys[head, (at + j) // TILE] = jnp.transpose(picked[j : j + TILE, :].astype(BF16))


def place_values(src, rows, heads, wide, vals, at):
    for head in range(heads):
        vals[head, at : at + rows, :] = one_head_rows(src, 0, rows, heads, wide, head).astype(BF16)


def id_column(ids, tile):
    return jnp.transpose(jnp.broadcast_to(ids[tile : tile + 1, :].astype(F32), (TILE, TILE)))


def id_row(ids, tile):
    return jnp.broadcast_to(ids[tile : tile + 1, :].astype(F32), (TILE, TILE))


def choose_kernel(kv_local, far_k, far_v, other_k, other_v, out, wide, own_k, own_v, sems):
    moves = [
        pltpu.make_async_copy(far_k, own_k, sems.at[0]),
        pltpu.make_async_copy(far_v, own_v, sems.at[1]),
    ]
    for move in moves:
        move.start()
    for move in moves:
        move.wait()
    positions = out.shape[0] // (4 * kv_local)
    heads = own_k.shape[0] // positions
    start = lax.axis_index("pair") * kv_local
    place = 0
    for mine, other in ((own_k, other_k), (own_v, other_v)):
        for slot, src in enumerate((mine, other)):
            wide[slot] = src[...].astype(F32)
        for head in range(kv_local):
            halves = [
                wide[slot, pl.ds(start + head, positions, stride=heads), :].astype(BF16)
                for slot in range(2)
            ]
            tile = jnp.concatenate(halves, axis=0)
            if mine is own_k:
                tile = jnp.transpose(tile)
            out[place : place + TILE, :] = tile
            place += TILE


def attend(
    q, keys, vals, raw, spans, masked, bias, factor, old, keep, emit, unroll, scores, peaks, tops, weights
):
    qheads, rows, _ = q.shape
    blocks = len(spans)
    group = qheads // keys.shape[0]

    for j, (low, high) in enumerate(spans):
        for first, end in ((0, low), (high, rows)):
            if first < end:
                weights[:, j, first:end, :] = jnp.zeros((2, end - first, TILE), BF16)

    def score(head, slot):
        kv = head // group
        if raw is None:
            wall = jnp.concatenate([keys[kv, j] for j in range(blocks)], axis=1)
            found = jnp.dot(q[head], wall, preferred_element_type=F32)
        best = {}
        for j, (low, high) in enumerate(spans):
            for first in range(low, high, TILE):
                part = slice(first, first + TILE)
                if raw is None:
                    piece = found[part, j * TILE : (j + 1) * TILE] * factor
                else:
                    piece = raw[head, j, part, :]
                if j < masked:
                    piece = piece + bias[j, part, :]
                scores[slot, j, part, :] = piece
                best[first] = jnp.maximum(best[first], piece) if first in best else piece
        for first, peak in best.items():
            peaks[slot, first : first + TILE, :] = peak

    def weigh(head, slot):
        for r in range(0, rows, CHUNK):
            part = slice(r, r + CHUNK)
            top = jnp.max(peaks[slot, part, :], axis=1, keepdims=True)
            top = jnp.broadcast_to(top, (CHUNK, TILE))
            if old is not None:
                top = jnp.maximum(top, old[head, part, :])
            if keep is None:
                tops[slot, part, :] = top
            else:
                keep[head, part, :] = top
            for j, (low, high) in enumerate(spans):
                if low <= r < high:
                    shifted = scores[slot, j, part, :] - top
                    weights[slot, j, part, :] = jnp.exp2(shifted).astype(BF16)

    def mix(head, slot):
        wall = jnp.concatenate([weights[slot, j] for j in range(blocks)], axis=1)
        mine = vals[head // group]
        mine = jnp.concatenate([mine, jnp.ones_like(mine)], axis=1)
        mixed = jnp.dot(wall, mine, preferred_element_type=F32)
        emit(head, tops[slot] if keep is None else keep[head], mixed)

    def step(head, slot):
        score(head + 1, 1 - slot)
        weigh(head, slot)
        mix(head - 1, 1 - slot)

    score(0, 0)
    score(1, 1)
    weigh(0, 0)
    trips = (qheads - 2) // unroll

    def trip(index, _):
        for ahead in range(1, unroll + 1):
            step(unroll * index + ahead, ahead % 2)
        return 0

    lax.fori_loop(0, trips, trip, 0)
    for head in range(1 + unroll * trips, qheads - 1):
        step(head, head % 2)
    last = qheads - 1
    weigh(last, last % 2)
    mix(last - 1, (last - 1) % 2)
    mix(last, last % 2)


def ahead_kernel(kv_local, rows, factor, q, k2, out, keys, wide):
    group = q.shape[0] // kv_local
    blocks = rows // TILE

    def one_head(head, _):
        kv = head // group
        wall = jnp.concatenate([keys[kv, j] for j in range(blocks)], axis=1)
        found = jnp.dot(q[head], wall, preferred_element_type=F32)
        for j in range(blocks):
            high = (j + 1) * TILE
            out[head, j, 0:high, :] = found[0:high, j * TILE : high] * factor
        return 0

    @pl.when(lax.axis_index("ctx") >= 2)
    def _():
        place_keys(k2, rows, kv_local, wide, keys, 0)
        lax.fori_loop(0, q.shape[0], one_head, 0, unroll=True)


def ahead(queries, k2, kv_local, factor):
    qheads, rows, width = queries.shape
    blocks = rows // TILE
    return pl.pallas_call(
        functools.partial(ahead_kernel, kv_local, rows, factor),
        out_shape=jax.ShapeDtypeStruct((qheads, blocks, rows, TILE), F32),
        in_specs=[VM] * 2,
        out_specs=VM,
        scratch_shapes=[
            pltpu.VMEM((kv_local, blocks, width, TILE), BF16),
            pltpu.VMEM((rows * kv_local, width), F32),
        ],
        cost_estimate=pl.CostEstimate(
            flops=2 * rows * qheads * rows * width, bytes_accessed=2**20, transcendentals=0
        ),
        compiler_params=pltpu.CompilerParams(vmem_limit_bytes=GRANT),
        name="ahead",
    )(queries, k2)


def absorb_kernel(plan, kv_local, rows, factor, *refs):
    refs = list(refs)
    q, ids = refs.pop(0), refs.pop(0)
    started, final = plan["old"], plan["final"]
    acc = refs.pop(0) if started else None
    stat = refs.pop(0) if started else None
    sources = [(kind, [refs.pop(0) for _ in range(taken)]) for kind, taken in plan["parts"]]
    outs = [refs.pop(0) for _ in range(1 if final else 2)]
    moves = []
    if not started:
        landed, k_here, v_here, sems = refs.pop(0), *refs[-3:]
        refs = refs[:-3]
        (kind, (k_far, v_far)) = sources[0]
        sources[0] = (kind, (k_here, v_here))
        moves = [
            pltpu.make_async_copy(k_far, k_here, sems.at[0]),
            pltpu.make_async_copy(v_far, v_here, sems.at[1]),
            pltpu.make_async_copy(q, landed, sems.at[2]),
        ]
        for move in moves:
            move.start()
        q = landed
    raw = None
    if plan["skips"]:
        acc, stat = outs
        raw = sources[0][1][0]
    if final:
        ready, leaving = refs[-2:]
        refs = refs[:-2]
    keys, vals, wide, bias, *room = refs

    def visible_at_all():
        source = sources[0][1][1]
        last = source[rows * kv_local : rows * kv_local + IDROWS, :].astype(F32)
        apart = last[rows // TILE - 1 : rows // TILE, TILE - 1 :] - ids[...].astype(F32)[0:1, 0:1]
        return (lax.axis_index("ctx") >= 2) & (jnp.max(jnp.abs(apart)) < 0.5)

    def work():
        tiles = rows // TILE
        mine = ids[...]
        at = 0
        masked = 0
        places, spans = [], []
        for kind, taken in sources:
            places.append((kind == "own", at, kind, taken))
            if kind == "prefix":
                size = sum(chunk.shape[0] for chunk in taken) // (2 * kv_local)
            else:
                size = rows
            for first in range(0, size, TILE):
                low = first if kind == "own" else 0
                high = first + TILE if kind == "back2" else rows
                spans.append((low, high))
            at += size
            if kind != "prefix":
                masked = at // TILE
        for own, at, kind, taken in sorted(places, key=lambda place: place[:2]):
            if kind == "prefix":
                size = 2 * kv_local * TILE
                for chunk in taken:
                    for first in range(0, chunk.shape[0], size):
                        for head in range(kv_local):
                            low = first + head * TILE
                            keys[head, at // TILE] = chunk[low : low + TILE, :]
                            low = first + (kv_local + head) * TILE
                            vals[head, at : at + TILE, :] = chunk[low : low + TILE, :]
                        at += TILE
                continue
            if kind == "own":
                other = mine
                spot = lax.broadcasted_iota(jnp.int32, (TILE, TILE), 0)
                place = lax.broadcasted_iota(jnp.int32, (TILE, TILE), 1)
            else:
                hops = 1 if kind == "back1" else 2
                other = taken[1][rows * kv_local : rows * kv_local + IDROWS, :].astype(F32)
                other = jnp.where(lax.axis_index("ctx") >= hops, other, 0.0)
            for i in range(tiles):
                column = id_column(mine, i)
                part = slice(i * TILE, (i + 1) * TILE)
                for j in range(tiles):
                    low, high = spans[at // TILE + j]
                    if not low <= i * TILE < high:
                        continue
                    seen = column == id_row(other, j)
                    if kind == "own" and j == i:
                        seen = seen & (place <= spot)
                    bias[at // TILE + j, part, :] = jnp.where(seen, 0.0, HIDDEN)
            if own:
                moves[0].wait()
                moves[1].wait()
            if not plan["skips"]:
                place_keys(taken[0], rows, kv_local, wide, keys, at)
            place_values(taken[1], rows, kv_local, wide, vals, at)

        def emit(head, top, mixed):
            upper, lower = mixed[:, 0:TILE], mixed[:, TILE:]
            if started:
                fade = jnp.exp2(stat[head] - top)
                upper = acc[head, :, 0:TILE] * fade + upper
                lower = acc[head, :, TILE:] * fade + lower
            if final:
                ready[head] = (upper / lower).astype(BF16)
                pltpu.make_async_copy(ready.at[head], outs[0].at[head], leaving.at[head]).start()
            else:
                outs[0][head, :, 0:TILE] = upper
                outs[0][head, :, TILE:] = lower
                if started:
                    outs[1][head] = top

        if not started:
            moves[2].wait()
        keep = None if final or plan["skips"] else outs[1]
        attend(q, keys, vals, raw, spans, masked, bias, factor, stat, keep, emit, 8 if final or plan["skips"] else 4, *room)

    if plan["skips"]:
        pl.when(visible_at_all())(work)
    else:
        work()
    if final:
        for head in range(q.shape[0]):
            pltpu.make_async_copy(ready.at[head], outs[0].at[head], leaving.at[head]).wait()


def absorb(parts, final, queries, ids, state, kv_local, factor):
    qheads, rows, width = queries.shape
    total = 0
    masked = 0
    for kind, arrays in parts:
        total += sum(a.shape[0] for a in arrays) // (2 * kv_local) if kind == "prefix" else rows
        masked = masked if kind == "prefix" else total
    plan = {
        "old": bool(state),
        "final": final,
        "skips": [kind for kind, _ in parts] == ["back2"] and not final,
        "parts": [(kind, len(arrays)) for kind, arrays in parts],
    }
    operands = [queries, ids, *state]
    for kind, arrays in parts:
        operands.extend(arrays)
    if final:
        shape = (jax.ShapeDtypeStruct((qheads, rows, width), BF16),)
    else:
        shape = (
            jax.ShapeDtypeStruct((qheads, rows, 2 * TILE), F32),
            jax.ShapeDtypeStruct((qheads, rows, TILE), F32),
        )
    specs = [VM] * len(operands)
    extra = []
    if not state:
        for at in (0, 2, 3):
            operands[at] = pltpu.with_memory_space_constraint(operands[at], pltpu.HBM)
        specs = [HB, VM, HB, HB] + [VM] * (len(operands) - 4)
        shape += (jax.ShapeDtypeStruct(queries.shape, BF16),)
        block = pltpu.VMEM(parts[0][1][0].shape, BF16)
        extra = [block, block, pltpu.SemaphoreType.DMA((3,))]
    out_specs = (VM,) * len(shape)
    aliases = {}
    if final:
        out_specs = (HB,)
        extra = [pltpu.VMEM(shape[0].shape, BF16), pltpu.SemaphoreType.DMA((qheads,))]
    elif plan["skips"]:
        aliases = {2: 0, 3: 1}
    return pl.pallas_call(
        functools.partial(absorb_kernel, plan, kv_local, rows, factor),
        out_shape=shape,
        in_specs=specs,
        out_specs=out_specs,
        input_output_aliases=aliases,
        scratch_shapes=[
            pltpu.VMEM((kv_local, total // TILE, width, TILE), BF16),
            pltpu.VMEM((kv_local, total, width), BF16),
            pltpu.VMEM((rows * kv_local, width), F32),
            pltpu.VMEM((max(masked, TILE) // TILE, rows, TILE), F32),
            *working_room(rows, total),
            *extra,
        ],
        cost_estimate=pl.CostEstimate(
            flops=4 * rows * qheads * total * width,
            bytes_accessed=4 * 2**20,
            transcendentals=rows * qheads * total,
        ),
        compiler_params=pltpu.CompilerParams(vmem_limit_bytes=GRANT),
    )(*operands)


def working_room(rows, total):
    return [
        pltpu.VMEM((2, total // TILE, rows, TILE), F32),
        pltpu.VMEM((2, rows, TILE), F32),
        pltpu.VMEM((2, rows, TILE), F32),
        pltpu.VMEM((2, total // TILE, rows, TILE), BF16),
    ]


def shards(query_suffix, key_suffix, value_suffix, key_prefix, value_prefix, file_ids):
    rows, _, width = query_suffix.shape
    kv_local = key_suffix.shape[1]
    factor = math.log2(math.e) / math.sqrt(width)
    count = lax.axis_size("ctx")
    queries = query_suffix.transpose(1, 0, 2)
    k0 = key_suffix.reshape(rows * kv_local, width)
    v0 = value_suffix.reshape(rows * kv_local, width)
    ids = (file_ids + 1).astype(BF16).reshape(rows // TILE, TILE)
    ids = jnp.pad(ids, ((0, IDROWS - rows // TILE), (0, 0)))
    k1 = passed_on(k0, 1)
    v1 = passed_on(jnp.concatenate([v0, ids]), 1)
    kp = key_prefix.reshape(-1, width)
    vp = value_prefix.reshape(-1, width)
    kp_other = swapped(kp, "pair", 1)
    vp_other = swapped(vp, "pair", 1)
    positions = key_prefix.shape[0]
    mine = pl.pallas_call(
        functools.partial(choose_kernel, kv_local),
        out_shape=jax.ShapeDtypeStruct((4 * kv_local * positions, width), BF16),
        in_specs=[HB, HB, VM, VM],
        out_specs=VM,
        scratch_shapes=[
            pltpu.VMEM((2,) + kp.shape, F32),
            pltpu.VMEM(kp.shape, BF16),
            pltpu.VMEM(vp.shape, BF16),
            pltpu.SemaphoreType.DMA((2,)),
        ],
        cost_estimate=pl.CostEstimate(flops=0, bytes_accessed=4 * kp.size * 2, transcendentals=0),
        compiler_params=pltpu.CompilerParams(vmem_limit_bytes=GRANT),
        name="choose",
    )(
        pltpu.with_memory_space_constraint(kp, pltpu.HBM),
        pltpu.with_memory_space_constraint(vp, pltpu.HBM),
        kp_other,
        vp_other,
    )
    k2 = passed_on(k1, 2)
    v2 = passed_on(v1, 2)
    prefix, arrived = [mine], []
    bit = count // 2
    while bit:
        groups = [prefix[:1], prefix[1:]] if bit == 1 else [prefix]
        for group in groups:
            whole = jnp.concatenate(group) if len(group) > 1 else group[0]
            arrived.append(swapped(whole, "ctx", bit))
        prefix = prefix + arrived
        arrived = []
        bit //= 2
    rest = (kv_local, factor)
    *state, queries = absorb([("own", [k0, v0])], False, queries, ids, (), *rest)
    args = (queries, ids)
    near = [("back1", [k1, v1]), ("prefix", prefix[:-1])]
    state = absorb(near, False, *args, state, *rest)
    raw = ahead(queries, k2, kv_local, factor)
    state = absorb([("back2", [raw, v2])], False, *args, state, *rest)
    (out,) = absorb([("prefix", prefix[-1:])], True, *args, state, *rest)
    return out.transpose(1, 0, 2)


def solution(mesh):
    in_specs = (
        P(("groups", "ctx"), ("head", "pair"), None),
        P(("groups", "ctx"), ("head", "pair"), None),
        P(("groups", "ctx"), ("head", "pair"), None),
        P(("groups", "ctx", "pair"), "head", None),
        P(("groups", "ctx", "pair"), "head", None),
        P(("groups", "ctx")),
    )
    out_specs = P(("groups", "ctx"), ("head", "pair"), None)

    return jax.shard_map(shards, mesh=mesh, in_specs=in_specs, out_specs=out_specs, check_vma=False)
```

```python
import functools
import math

import jax
import jax.numpy as jnp
from jax import lax
from jax.experimental import pallas as pl
from jax.experimental.pallas import tpu as pltpu
from jax.sharding import PartitionSpec as P


HIDDEN = -1e30
TILE = 128
IDROWS = 16
CHUNK = 32
GRANT = 24 * 2**20
F32 = jnp.float32
BF16 = jnp.bfloat16
VM = pl.BlockSpec(memory_space=pltpu.VMEM)
HB = pl.BlockSpec(memory_space=pltpu.HBM)


def passed_on(value, hop):
    count = lax.axis_size("ctx")
    if hop == 1:
        pairs = [(i, (i + 1) % count) for i in range(count)]
    else:
        pairs = [(i, i + 1) for i in range(hop - 1, count - 1)]
    return lax.ppermute(value, "ctx", pairs)


def swapped(value, axis, bit):
    count = lax.axis_size(axis)
    return lax.ppermute(value, axis, [(i, i ^ bit) for i in range(count)])


def one_head_rows(src, first, rows, heads, wide, head):
    if head == 0:
        wide[0 : rows * heads, :] = src[first : first + rows * heads, :].astype(F32)
    return wide[pl.ds(head, rows, stride=heads), :]


def place_keys(src, rows, heads, wide, keys, at):
    for head in range(heads):
        picked = one_head_rows(src, 0, rows, heads, wide, head)
        for j in range(0, rows, TILE):
            keys[head, (at + j) // TILE] = jnp.transpose(picked[j : j + TILE, :].astype(BF16))


def place_values(src, rows, heads, wide, vals, at):
    for head in range(heads):
        vals[head, at : at + rows, :] = one_head_rows(src, 0, rows, heads, wide, head).astype(BF16)


def id_column(ids, tile):
    return jnp.transpose(jnp.broadcast_to(ids[tile : tile + 1, :].astype(F32), (TILE, TILE)))


def id_row(ids, tile):
    return jnp.broadcast_to(ids[tile : tile + 1, :].astype(F32), (TILE, TILE))


def choose_kernel(kv_local, far_k, far_v, other_k, other_v, out, wide, own_k, own_v, sems):
    moves = [
        pltpu.make_async_copy(far_k, own_k, sems.at[0]),
        pltpu.make_async_copy(far_v, own_v, sems.at[1]),
    ]
    for move in moves:
        move.start()
    for move in moves:
        move.wait()
    positions = out.shape[0] // (4 * kv_local)
    heads = own_k.shape[0] // positions
    start = lax.axis_index("pair") * kv_local
    place = 0
    for mine, other in ((own_k, other_k), (own_v, other_v)):
        for slot, src in enumerate((mine, other)):
            wide[slot] = src[...].astype(F32)
        for head in range(kv_local):
            halves = [
                wide[slot, pl.ds(start + head, positions, stride=heads), :].astype(BF16)
                for slot in range(2)
            ]
            tile = jnp.concatenate(halves, axis=0)
            if mine is own_k:
                tile = jnp.transpose(tile)
            out[place : place + TILE, :] = tile
            place += TILE


def attend(
    q, keys, vals, raw, spans, masked, bias, factor, old, keep, emit, unroll, scores, peaks, tops, weights
):
    qheads, rows, _ = q.shape
    blocks = len(spans)
    plain = masked == 0
    group = qheads // keys.shape[0]

    for j, (low, high) in enumerate(spans):
        for first, end in ((0, low), (high, rows)):
            if first < end:
                weights[:, j, first:end, :] = jnp.zeros((2, end - first, TILE), BF16)

    def score(head, slot):
        kv = head // group
        if raw is None:
            wall = jnp.concatenate([keys[kv, j] for j in range(blocks)], axis=1)
            found = jnp.dot(q[head], wall, preferred_element_type=F32)
        best = {}
        for j, (low, high) in enumerate(spans):
            for first in range(low, high, TILE):
                part = slice(first, first + TILE)
                if raw is None:
                    piece = found[part, j * TILE : (j + 1) * TILE]
                    piece = piece if plain else piece * factor
                else:
                    piece = raw[head, j, part, :]
                if j < masked:
                    piece = piece + bias[j, part, :]
                scores[slot, j, part, :] = piece
                best[first] = jnp.maximum(best[first], piece) if first in best else piece
        for first, peak in best.items():
            peaks[slot, first : first + TILE, :] = peak

    def weigh(head, slot):
        for r in range(0, rows, CHUNK):
            part = slice(r, r + CHUNK)
            top = jnp.max(peaks[slot, part, :], axis=1, keepdims=True)
            top = jnp.broadcast_to(top, (CHUNK, TILE))
            top = top * factor if plain else top
            if old is not None:
                top = jnp.maximum(top, old[head, part, :])
            if keep is None:
                tops[slot, part, :] = top
            else:
                keep[head, part, :] = top
            for j, (low, high) in enumerate(spans):
                if low <= r < high:
                    value = scores[slot, j, part, :]
                    shifted = (value * factor if plain else value) - top
                    weights[slot, j, part, :] = jnp.exp2(shifted).astype(BF16)

    def mix(head, slot):
        wall = jnp.concatenate([weights[slot, j] for j in range(blocks)], axis=1)
        mine = vals[head // group]
        mine = jnp.concatenate([mine, jnp.ones_like(mine)], axis=1)
        mixed = jnp.dot(wall, mine, preferred_element_type=F32)
        emit(head, tops[slot] if keep is None else keep[head], mixed)

    def step(head, slot):
        score(head + 1, 1 - slot)
        weigh(head, slot)
        mix(head - 1, 1 - slot)

    score(0, 0)
    score(1, 1)
    weigh(0, 0)
    trips = (qheads - 2) // unroll

    def trip(index, _):
        for ahead in range(1, unroll + 1):
            step(unroll * index + ahead, ahead % 2)
        return 0

    lax.fori_loop(0, trips, trip, 0)
    for head in range(1 + unroll * trips, qheads - 1):
        step(head, head % 2)
    last = qheads - 1
    weigh(last, last % 2)
    mix(last - 1, (last - 1) % 2)
    mix(last, last % 2)


def ahead_kernel(kv_local, rows, factor, q, k2, out, keys, wide):
    group = q.shape[0] // kv_local
    blocks = rows // TILE

    def one_head(head, _):
        kv = head // group
        wall = jnp.concatenate([keys[kv, j] for j in range(blocks)], axis=1)
        found = jnp.dot(q[head], wall, preferred_element_type=F32)
        for j in range(blocks):
            high = (j + 1) * TILE
            out[head, j, 0:high, :] = found[0:high, j * TILE : high] * factor
        return 0

    @pl.when(lax.axis_index("ctx") >= 2)
    def _():
        place_keys(k2, rows, kv_local, wide, keys, 0)
        lax.fori_loop(0, q.shape[0], one_head, 0, unroll=True)


def ahead(queries, k2, kv_local, factor):
    qheads, rows, width = queries.shape
    blocks = rows // TILE
    return pl.pallas_call(
        functools.partial(ahead_kernel, kv_local, rows, factor),
        out_shape=jax.ShapeDtypeStruct((qheads, blocks, rows, TILE), F32),
        in_specs=[VM] * 2,
        out_specs=VM,
        scratch_shapes=[
            pltpu.VMEM((kv_local, blocks, width, TILE), BF16),
            pltpu.VMEM((rows * kv_local, width), F32),
        ],
        cost_estimate=pl.CostEstimate(
            flops=2 * rows * qheads * rows * width, bytes_accessed=2**20, transcendentals=0
        ),
        compiler_params=pltpu.CompilerParams(vmem_limit_bytes=GRANT),
        name="ahead",
    )(queries, k2)


def absorb_kernel(plan, kv_local, rows, factor, *refs):
    refs = list(refs)
    q, ids = refs.pop(0), refs.pop(0)
    started, final = plan["old"], plan["final"]
    acc = refs.pop(0) if started else None
    stat = refs.pop(0) if started else None
    sources = [(kind, [refs.pop(0) for _ in range(taken)]) for kind, taken in plan["parts"]]
    outs = [refs.pop(0) for _ in range(1 if final else 2)]
    moves = []
    if not started:
        landed, k_here, v_here, sems = refs.pop(0), *refs[-3:]
        refs = refs[:-3]
        (kind, (k_far, v_far)) = sources[0]
        sources[0] = (kind, (k_here, v_here))
        moves = [
            pltpu.make_async_copy(k_far, k_here, sems.at[0]),
            pltpu.make_async_copy(v_far, v_here, sems.at[1]),
            pltpu.make_async_copy(q, landed, sems.at[2]),
        ]
        for move in moves:
            move.start()
        q = landed
    raw = None
    if plan["skips"]:
        acc, stat = outs
        raw = sources[0][1][0]
    if final:
        ready, leaving = refs[-2:]
        refs = refs[:-2]
    keys, vals, wide, bias, *room = refs

    def visible_at_all():
        source = sources[0][1][1]
        last = source[rows * kv_local : rows * kv_local + IDROWS, :].astype(F32)
        apart = last[rows // TILE - 1 : rows // TILE, TILE - 1 :] - ids[...].astype(F32)[0:1, 0:1]
        return (lax.axis_index("ctx") >= 2) & (jnp.max(jnp.abs(apart)) < 0.5)

    def work():
        tiles = rows // TILE
        mine = ids[...]
        at = 0
        masked = 0
        places, spans = [], []
        for kind, taken in sources:
            places.append((kind == "own", at, kind, taken))
            if kind == "prefix":
                size = sum(chunk.shape[0] for chunk in taken) // (2 * kv_local)
            else:
                size = rows
            for first in range(0, size, TILE):
                low = first if kind == "own" else 0
                high = first + TILE if kind == "back2" else rows
                spans.append((low, high))
            at += size
            if kind != "prefix":
                masked = at // TILE
        for own, at, kind, taken in sorted(places, key=lambda place: place[:2]):
            if kind == "prefix":
                size = 2 * kv_local * TILE
                for chunk in taken:
                    for first in range(0, chunk.shape[0], size):
                        for head in range(kv_local):
                            low = first + head * TILE
                            keys[head, at // TILE] = chunk[low : low + TILE, :]
                            low = first + (kv_local + head) * TILE
                            vals[head, at : at + TILE, :] = chunk[low : low + TILE, :]
                        at += TILE
                continue
            if kind == "own":
                other = mine
                spot = lax.broadcasted_iota(jnp.int32, (TILE, TILE), 0)
                place = lax.broadcasted_iota(jnp.int32, (TILE, TILE), 1)
            else:
                hops = 1 if kind == "back1" else 2
                other = taken[1][rows * kv_local : rows * kv_local + IDROWS, :].astype(F32)
                other = jnp.where(lax.axis_index("ctx") >= hops, other, 0.0)
            for i in range(tiles):
                column = id_column(mine, i)
                part = slice(i * TILE, (i + 1) * TILE)
                for j in range(tiles):
                    low, high = spans[at // TILE + j]
                    if not low <= i * TILE < high:
                        continue
                    seen = column == id_row(other, j)
                    if kind == "own" and j == i:
                        seen = seen & (place <= spot)
                    bias[at // TILE + j, part, :] = jnp.where(seen, 0.0, HIDDEN)
            if own:
                moves[0].wait()
                moves[1].wait()
            if not plan["skips"]:
                place_keys(taken[0], rows, kv_local, wide, keys, at)
            place_values(taken[1], rows, kv_local, wide, vals, at)

        def emit(head, top, mixed):
            upper, lower = mixed[:, 0:TILE], mixed[:, TILE:]
            if started:
                fade = jnp.exp2(stat[head] - top)
                upper = acc[head, :, 0:TILE] * fade + upper
                lower = acc[head, :, TILE:] * fade + lower
            if final:
                ready[head] = (upper / lower).astype(BF16)
                pltpu.make_async_copy(ready.at[head], outs[0].at[head], leaving.at[head]).start()
            else:
                outs[0][head, :, 0:TILE] = upper
                outs[0][head, :, TILE:] = lower
                if started:
                    outs[1][head] = top

        if not started:
            moves[2].wait()
        keep = None if final or plan["skips"] else outs[1]
        attend(q, keys, vals, raw, spans, masked, bias, factor, stat, keep, emit, 8, *room)

    if plan["skips"]:
        pl.when(visible_at_all())(work)
    else:
        work()
    if final:
        for head in range(q.shape[0]):
            pltpu.make_async_copy(ready.at[head], outs[0].at[head], leaving.at[head]).wait()


def absorb(parts, final, queries, ids, state, kv_local, factor):
    qheads, rows, width = queries.shape
    total = 0
    masked = 0
    for kind, arrays in parts:
        total += sum(a.shape[0] for a in arrays) // (2 * kv_local) if kind == "prefix" else rows
        masked = masked if kind == "prefix" else total
    plan = {
        "old": bool(state),
        "final": final,
        "skips": [kind for kind, _ in parts] == ["back2"] and not final,
        "parts": [(kind, len(arrays)) for kind, arrays in parts],
    }
    operands = [queries, ids, *state]
    for kind, arrays in parts:
        operands.extend(arrays)
    if final:
        shape = (jax.ShapeDtypeStruct((qheads, rows, width), BF16),)
    else:
        shape = (
            jax.ShapeDtypeStruct((qheads, rows, 2 * TILE), F32),
            jax.ShapeDtypeStruct((qheads, rows, TILE), F32),
        )
    specs = [VM] * len(operands)
    extra = []
    if not state:
        for at in (0, 2, 3):
            operands[at] = pltpu.with_memory_space_constraint(operands[at], pltpu.HBM)
        specs = [HB, VM, HB, HB] + [VM] * (len(operands) - 4)
        shape += (jax.ShapeDtypeStruct(queries.shape, BF16),)
        block = pltpu.VMEM(parts[0][1][0].shape, BF16)
        extra = [block, block, pltpu.SemaphoreType.DMA((3,))]
    out_specs = (VM,) * len(shape)
    aliases = {}
    if final:
        out_specs = (HB,)
        extra = [pltpu.VMEM(shape[0].shape, BF16), pltpu.SemaphoreType.DMA((qheads,))]
    elif plan["skips"]:
        aliases = {2: 0, 3: 1}
    return pl.pallas_call(
        functools.partial(absorb_kernel, plan, kv_local, rows, factor),
        out_shape=shape,
        in_specs=specs,
        out_specs=out_specs,
        input_output_aliases=aliases,
        scratch_shapes=[
            pltpu.VMEM((kv_local, total // TILE, width, TILE), BF16),
            pltpu.VMEM((kv_local, total, width), BF16),
            pltpu.VMEM((rows * kv_local, width), F32),
            pltpu.VMEM((max(masked, TILE) // TILE, rows, TILE), F32),
            *working_room(rows, total),
            *extra,
        ],
        cost_estimate=pl.CostEstimate(
            flops=4 * rows * qheads * total * width,
            bytes_accessed=4 * 2**20,
            transcendentals=rows * qheads * total,
        ),
        compiler_params=pltpu.CompilerParams(vmem_limit_bytes=GRANT),
    )(*operands)


def working_room(rows, total):
    return [
        pltpu.VMEM((2, total // TILE, rows, TILE), F32),
        pltpu.VMEM((2, rows, TILE), F32),
        pltpu.VMEM((2, rows, TILE), F32),
        pltpu.VMEM((2, total // TILE, rows, TILE), BF16),
    ]


def shards(query_suffix, key_suffix, value_suffix, key_prefix, value_prefix, file_ids):
    rows, _, width = query_suffix.shape
    kv_local = key_suffix.shape[1]
    factor = math.log2(math.e) / math.sqrt(width)
    count = lax.axis_size("ctx")
    queries = query_suffix.transpose(1, 0, 2)
    k0 = key_suffix.reshape(rows * kv_local, width)
    v0 = value_suffix.reshape(rows * kv_local, width)
    ids = (file_ids + 1).astype(BF16).reshape(rows // TILE, TILE)
    ids = jnp.pad(ids, ((0, IDROWS - rows // TILE), (0, 0)))
    k1 = passed_on(k0, 1)
    v1 = passed_on(jnp.concatenate([v0, ids]), 1)
    kp = key_prefix.reshape(-1, width)
    vp = value_prefix.reshape(-1, width)
    kp_other = swapped(kp, "pair", 1)
    vp_other = swapped(vp, "pair", 1)
    positions = key_prefix.shape[0]
    mine = pl.pallas_call(
        functools.partial(choose_kernel, kv_local),
        out_shape=jax.ShapeDtypeStruct((4 * kv_local * positions, width), BF16),
        in_specs=[HB, HB, VM, VM],
        out_specs=VM,
        scratch_shapes=[
            pltpu.VMEM((2,) + kp.shape, F32),
            pltpu.VMEM(kp.shape, BF16),
            pltpu.VMEM(vp.shape, BF16),
            pltpu.SemaphoreType.DMA((2,)),
        ],
        cost_estimate=pl.CostEstimate(flops=0, bytes_accessed=4 * kp.size * 2, transcendentals=0),
        compiler_params=pltpu.CompilerParams(vmem_limit_bytes=GRANT),
        name="choose",
    )(
        pltpu.with_memory_space_constraint(kp, pltpu.HBM),
        pltpu.with_memory_space_constraint(vp, pltpu.HBM),
        kp_other,
        vp_other,
    )
    k2 = passed_on(k1, 2)
    v2 = passed_on(v1, 2)
    prefix, arrived = [mine], []
    bit = count // 2
    while bit:
        groups = [prefix[:1], prefix[1:]] if bit == 1 else [prefix]
        for group in groups:
            whole = jnp.concatenate(group) if len(group) > 1 else group[0]
            arrived.append(swapped(whole, "ctx", bit))
        prefix = prefix + arrived
        arrived = []
        bit //= 2
    rest = (kv_local, factor)
    *state, queries = absorb([("own", [k0, v0])], False, queries, ids, (), *rest)
    args = (queries, ids)
    near = [("back1", [k1, v1]), ("prefix", prefix[:-1])]
    state = absorb(near, False, *args, state, *rest)
    raw = ahead(queries, k2, kv_local, factor)
    state = absorb([("back2", [raw, v2])], False, *args, state, *rest)
    (out,) = absorb([("prefix", prefix[-1:])], True, *args, state, *rest)
    return out.transpose(1, 0, 2)


def solution(mesh):
    in_specs = (
        P(("groups", "ctx"), ("head", "pair"), None),
        P(("groups", "ctx"), ("head", "pair"), None),
        P(("groups", "ctx"), ("head", "pair"), None),
        P(("groups", "ctx", "pair"), "head", None),
        P(("groups", "ctx", "pair"), "head", None),
        P(("groups", "ctx")),
    )
    out_specs = P(("groups", "ctx"), ("head", "pair"), None)

    return jax.shard_map(shards, mesh=mesh, in_specs=in_specs, out_specs=out_specs, check_vma=False)
```
